128 devices in a mesh: dom: 8 (over z, core), blk: 16 (over y, x).
Axes of the slice: x: 4, y: 4, z: 4, core: 2. Of those that a mesh axis runs over, the one named last changes fastest.
Arguments:
- queries: bfloat16 [2048, 768], P(('dom', 'blk')), may hold values from -6 to 6
- adapter_w: bfloat16 [768, 768], replicated, may hold values from -0.21875 to 0.21875
- index_rows: bfloat16 [64, 8192, 768], P('dom', 'blk'), may hold values from -16 to 16
- probes: int32 [2048, 16], P(('dom', 'blk')), may hold values from 0 to 63, all different within a row; in each aligned block of 2048 rows (0 to 2047, 2048 to 4095, ...) at most 1024 rows name the same one
- list_slot: int32 [64], replicated, may hold values from 0 to 63, each once
- block_counts: int32 [64], replicated, may hold values from 48 to 64
- target_raw: int32 [2048], P(('dom', 'blk')), may hold values from 0 to 131071
Outputs:
- query_grad: bfloat16 [2048, 768], P(('dom', 'blk'))
- adapter_grad: float32 [768, 768], replicated
The draws below stay inside these ranges and needn't reach their ends.
Inputs may be any that keep to these rules, and one draw needn't show every extreme that they name: `probes`: each row names 16 different lists; at most 1024 queries name one list, a bound that some block reaches. `list_slot`: each list id once.
All inputs are finite; a program needn't handle non-finite values.
Results may differ from the reference program's by a relative error of at most 0.015.
Values may be sent and summed in bfloat16 or wider, within the bound.
No kernel may reach another device: no remote copies, remote signals or barrier semaphores. Data moves between devices by JAX's collectives and lax.ppermute only.
A program may use at most 128 MiB of HBM per device.

```python
import math
import jax
import jax.numpy as jnp
import numpy as np
from jax import lax

D = 768
QUERIES = 2048
PROBES = 16
LISTS = 64
ROWS = 128
NBL = 64
LROWS = 8192
CAP = 1024


special_gain = 6.0


def slot_directions(key):
    direction_key = jax.random.fold_in(key, 101)
    return jnp.clip(jax.random.normal(direction_key, (LISTS, D), jnp.float32), -2.0, 2.0)


def draw_queries(key, part):
    own_key = jax.random.fold_in(key, 11)
    first_key = jax.random.fold_in(own_key, 0)
    plant_key = jax.random.fold_in(own_key, 4)
    pick_key = jax.random.fold_in(own_key, 5)
    gap_key = jax.random.fold_in(own_key, 6)
    noise_key = jax.random.fold_in(own_key, 7)
    directions = slot_directions(key)
    planted = jax.random.uniform(plant_key, (QUERIES, 1), jnp.float32) < 0.25
    picked = jax.random.randint(pick_key, (QUERIES,), 0, LISTS)
    gap_size = jax.random.uniform(gap_key, (QUERIES, 1), jnp.float32, 9.0, 13.5)
    strength = gap_size / (special_gain * 0.92 * math.sqrt(D))
    small_noise = 0.03 * jnp.clip(jax.random.normal(noise_key, (QUERIES, D), jnp.float32), -3.0, 3.0)
    spiked = strength * directions[picked] + small_noise
    values = jnp.clip(jax.random.normal(first_key, (QUERIES, D), jnp.float32), -6.0, 6.0)
    values = jnp.where(planted, spiked, values)
    return values.astype(jnp.bfloat16)


def draw_index_rows(key, part):
    own_key = jax.random.fold_in(key, 23)
    first_key, scale_key, common_key = jax.random.split(own_key, 3)
    directions = slot_directions(key)
    row_scale = jnp.exp(jax.random.uniform(scale_key, (LISTS, LROWS, 1), jnp.float32, math.log(0.25), math.log(2.5)))
    common = jnp.clip(2.0 * jax.random.normal(common_key, (1, 1, D), jnp.float32), -3.5, 3.5)
    row_pos = jnp.arange(LROWS)[None, :, None]
    special = special_gain * directions[:, None, :] + common
    values = jnp.clip(jax.random.normal(first_key, (LISTS, LROWS, D), jnp.float32), -3.0, 3.0) * row_scale + common
    values = jnp.where(row_pos == 2, special, values)
    return values.astype(jnp.bfloat16)


def plant(drawn, stream_key, low, top_value):
    index_at = [jax.random.randint(jax.random.fold_in(stream_key, axis), (), 0, length) for axis, length in enumerate(drawn.shape)]
    main_axis = drawn.shape.index(max(drawn.shape))
    next_to = index_at[:main_axis] + [(index_at[main_axis] + 1) % drawn.shape[main_axis]] + index_at[main_axis + 1:]
    return drawn.at[tuple(index_at)].set(low).at[tuple(next_to)].set(top_value)


def assign_block(stream_key, own, number, rows, count, top, most, lean):
    order = jax.random.permutation(stream_key, count)
    heavy_load, usual = shares(count, rows * top, most, lean, True), shares(count, rows * top, most, lean, False)
    places = jnp.arange(count)

    def named(sizes, offset_by):
        used = int((sizes > 0).sum())
        fixed = max(1, used // 4)
        moved = fixed + (places - fixed + offset_by * (used - fixed)) % max(1, count - fixed)
        return jnp.zeros((count,), jnp.int32).at[order[jnp.where(places < fixed, places, moved)]].set(jnp.asarray(sizes, jnp.int32))

    sizes = jnp.where(number % 4 == 0, named(heavy_load, number // 4), named(usual, number - number // 4 - 1))
    mixed = jax.random.permutation(jax.random.fold_in(own, 3), count)
    giver, receiver = mixed[0:count // 2 * 2:2], mixed[1:count // 2 * 2:2]
    room = jnp.minimum(sizes[giver] - 1, most - sizes[receiver]) // 2
    room = jnp.where((giver == order[0]) | (receiver == order[0]) | (sizes[receiver] == 0), 0, jnp.maximum(room, 0))
    moved = jax.random.randint(jax.random.fold_in(own, 4), (count // 2,), 0, 1 << 20) % (room + 1)
    sizes = sizes.at[giver].add(-moved).at[receiver].add(moved)
    items = jnp.searchsorted(jnp.cumsum(sizes), jnp.arange(rows * top), side="right").astype(jnp.int32)
    table = items.reshape(top, rows).T
    table = table[jax.random.permutation(jax.random.fold_in(own, 1), rows)]
    offset_by = jax.random.randint(jax.random.fold_in(own, 2), (rows, 1), 0, top)
    return jnp.take_along_axis(table, (jnp.arange(top)[None, :] + offset_by) % top, axis=1)


def shares(number_of, total, limit, lean, full):
    portions = [(1 << 20) // math.isqrt(standing ** lean) + 1 for standing in range(1, number_of + 1)]
    largest = limit if full else min(limit, max(-(-total // number_of), total * portions[0] // sum(portions)))
    least = 1 if total - largest >= number_of - 1 else 0
    counts, surplus = [largest] + [least] * (number_of - 1), total - largest - least * (number_of - 1)
    while surplus > 0:
        movable = [i for i in range(1, number_of) if counts[i] < largest] or [i for i in range(1, number_of) if counts[i] < limit]
        pool, remaining = sum([portions[i] for i in movable]), surplus
        for i in movable:
            addition = min(limit - counts[i], max(1, remaining * portions[i] // pool), surplus)
            counts[i] = counts[i] + addition
            surplus = surplus - addition
    return np.array(counts)


def gaussian(key, shape, width, reach, kind=jnp.bfloat16):
    result = width * jax.random.normal(key, shape, jnp.float32)
    return jnp.clip(result, min=-reach, max=reach).astype(kind)


def setup_inputs(seed: int = 0) -> dict:
    seeds = jax.random.split(jax.random.key(seed), 8)
    queries = draw_queries(jax.random.fold_in(seeds[7], 71), 0)
    adapter_w = gaussian(seeds[1], (D, D), D ** -0.5, 0.21875)
    index_rows = draw_index_rows(jax.random.fold_in(seeds[7], 71), 0)
    probes_keys = jax.random.split(jax.random.fold_in(seeds[3], 1), QUERIES // QUERIES)
    probes_turns = jax.random.permutation(jax.random.fold_in(seeds[3], 3), QUERIES // QUERIES)
    probes = jax.vmap(lambda own, number: assign_block(jax.random.fold_in(seeds[3], 2), own, number, QUERIES, LISTS, PROBES, CAP, 2))(probes_keys, probes_turns).reshape((QUERIES, PROBES))
    list_slot = jax.random.permutation(seeds[4], LISTS).astype(jnp.int32)
    block_counts = plant(jax.random.randint(seeds[5], (LISTS,), NBL - NBL // 4, NBL + 1), jax.random.fold_in(seeds[5], 1), NBL - NBL // 4, NBL).astype(jnp.int32)
    target_raw = plant(jax.random.randint(seeds[6], (QUERIES,), 0, PROBES * LROWS), jax.random.fold_in(seeds[6], 1), 0, (PROBES * LROWS) - 1).astype(jnp.int32)
    return dict(queries=queries, adapter_w=adapter_w, index_rows=index_rows, probes=probes, list_slot=list_slot, block_counts=block_counts, target_raw=target_raw)


NEG_FILL = -1e+30

def table_lookup(small_table, lookup_keys):
    matches = lookup_keys[..., None] == jnp.arange(small_table.shape[0], dtype=jnp.int32)
    return lax.optimization_barrier(jnp.sum(jnp.where(matches, small_table, 0), axis=-1)).astype(jnp.int32)

def select_slots(probe_mask, capacity):
    count_all = probe_mask.shape[0]
    position = (jnp.cumsum(probe_mask.astype(jnp.int32)) - 1).astype(jnp.int32)
    position = jnp.where(probe_mask, position, capacity).astype(jnp.int32)
    filled = jnp.zeros((capacity,), jnp.int32).at[position].set(jnp.arange(count_all, dtype=jnp.int32), mode='drop')
    used = jnp.sum(probe_mask.astype(jnp.int32)).astype(jnp.int32)
    slot_valid = jnp.arange(capacity, dtype=jnp.int32) < used
    scatter_rows = jnp.where(slot_valid, filled, count_all).astype(jnp.int32)
    return (filled, slot_valid, scatter_rows)

def reference(queries, adapter_w, index_rows, probes, list_slot, block_counts, target_raw):
    score_scale = 1.0 / math.sqrt(D)
    adapted = (queries.astype(jnp.float32) + jnp.dot(queries, adapter_w, preferred_element_type=jnp.float32)).astype(jnp.bfloat16)
    stored = table_lookup(list_slot, probes)
    which_probe = (target_raw // LROWS).astype(jnp.int32)
    target_list = jnp.take_along_axis(probes, which_probe[:, None], axis=1)[:, 0]
    target_slot = table_lookup(list_slot, target_list)
    target_row = (target_raw % LROWS % (ROWS * table_lookup(block_counts, target_list))).astype(jnp.int32)
    row_ids = jnp.arange(LROWS, dtype=jnp.int32)

    def list_scores(slot_id):
        probe_mask = jnp.any(stored == slot_id, axis=1)
        filled, slot_valid, scatter_rows = select_slots(probe_mask, CAP)
        chosen = adapted[filled]
        list_rows = lax.dynamic_index_in_dim(index_rows, slot_id, 0, keepdims=False)
        live_rows = (ROWS * jnp.sum(jnp.where(list_slot == slot_id, block_counts, 0))).astype(jnp.int32)
        raw_scores = lax.dot_general(chosen, list_rows, (((1,), (1,)), ((), ())), preferred_element_type=jnp.float32) * score_scale
        keep_entry = slot_valid[:, None] & (row_ids[None, :] < live_rows)
        return (jnp.where(keep_entry, raw_scores, NEG_FILL), filled, slot_valid, scatter_rows, list_rows)

    def first_pass(slot_id):
        scores, filled, slot_valid, scatter_rows, list_rows = list_scores(slot_id)
        row_top = lax.optimization_barrier(jnp.max(scores, axis=1))
        row_sum = jnp.where(slot_valid, lax.optimization_barrier(jnp.sum(jnp.exp(scores - row_top[:, None]), axis=1)), 0.0)
        return (row_top, row_sum, scatter_rows)
    list_tops, list_sums, list_scatter = lax.map(first_pass, jnp.arange(LISTS, dtype=jnp.int32))
    top_score = jnp.full((QUERIES,), NEG_FILL, jnp.float32).at[list_scatter.ravel()].max(list_tops.ravel(), mode='drop')
    read_rows = jnp.minimum(list_scatter, QUERIES - 1)
    rescaled = list_sums * jnp.exp(list_tops - top_score[read_rows])
    score_total = jnp.zeros((QUERIES,), jnp.float32).at[list_scatter.ravel()].add(rescaled.ravel(), mode='drop')

    def second_pass(back_sum, slot_id):
        scores, filled, slot_valid, scatter_rows, list_rows = list_scores(slot_id)
        softmax_weight = jnp.exp(scores - top_score[filled][:, None]) / score_total[filled][:, None]
        is_target = slot_valid[:, None] & (target_slot[filled] == slot_id)[:, None] & (target_row[filled][:, None] == row_ids[None, :])
        score_grad = (softmax_weight - is_target.astype(jnp.float32)).astype(jnp.bfloat16)
        back_part = jnp.dot(score_grad, list_rows, preferred_element_type=jnp.float32) * score_scale
        return (back_sum.at[scatter_rows].add(back_part, mode='drop'), None)
    back, ignored = lax.scan(second_pass, jnp.zeros((QUERIES, D), jnp.float32), jnp.arange(LISTS, dtype=jnp.int32))
    back_low = back.astype(jnp.bfloat16)
    query_grad = (back + lax.dot_general(back_low, adapter_w, (((1,), (1,)), ((), ())), preferred_element_type=jnp.float32)).astype(jnp.bfloat16)
    adapter_grad = lax.dot_general(queries, back_low, (((0,), (0,)), ((), ())), preferred_element_type=jnp.float32) * (1.0 / math.sqrt(QUERIES))
    return (query_grad, adapter_grad)
```

```python
import functools
import math

import jax
import jax.numpy as jnp
from jax import lax
from jax.experimental import pallas as pl
from jax.experimental.pallas import tpu as pltpu
from jax.sharding import Mesh
from jax.sharding import PartitionSpec as P

ROWS = 128
NEG_FILL = -1e30
LANES = 128
SIZES = (4, 2, 4, 4)
AXES = ("z", "core", "y", "x")


def table_lookup(small_table, lookup_keys):
    matches = lookup_keys[..., None] == jnp.arange(small_table.shape[0], dtype=jnp.int32)
    return jnp.sum(jnp.where(matches, small_table, 0), axis=-1)


def from_ahead(value, axis, step):
    size = lax.axis_size(axis)
    return lax.ppermute(value, axis, [((i + step) % size, i) for i in range(size)])


def gather_axis(value, axis):
    size = lax.axis_size(axis)
    return jnp.concatenate([value] + [from_ahead(value, axis, j) for j in range(1, size)], axis=0)


def gather_all(value):
    for axis in ("x", "y", "z", "core"):
        value = gather_axis(value, axis)
    return value


def tile_of(i, place):
    return (lax.rem(i, 2) ^ place[1]) * 4 + lax.rem(i // 2 - place[0] + 4, 4)


def reorder_tile(source, target, place, width):
    for y in range(4):
        for x in range(4):
            at = lax.rem(y - place[2] + 4, 4) * 4 + lax.rem(x - place[3] + 4, 4)
            block = source[pl.ds(pl.multiple_of(at * 16, 16), 16), :]
            target[(y * 4 + x) * 16 : (y * 4 + x) * 16 + 16, :] = block[:, :width]


def score_kernel(place, live, packed_ref, w_ref, rows_ref, q_ref, info_ref, p_ref, stats_ref, own, s_ref):
    width = w_ref.shape[0]
    scale = 1.0 / math.sqrt(width)
    reorder_tile(packed_ref, own, place, own.shape[1])
    queries = own[:, :width]
    q_ref[...] = queries
    info = own[:, width:]
    info_ref[...] = info
    adapted = (
        queries.astype(jnp.float32) + jnp.dot(queries, w_ref[...], preferred_element_type=jnp.float32)
    ).astype(jnp.bfloat16)
    tile = adapted.shape[0]
    lane = lax.broadcasted_iota(jnp.int32, (tile, LANES), 1)
    slots = jnp.where(lane < 16, info.astype(jnp.float32), -1.0)
    top = jnp.full((tile, LANES), -3e38, jnp.float32)
    lists = rows_ref.shape[0]
    per = rows_ref.shape[1]
    for j in range(lists):
        slot = (place[4] + j).astype(jnp.float32)
        probed = jnp.max(jnp.where(slots == slot, 1.0, 0.0), axis=1, keepdims=True)
        bias = jnp.broadcast_to(jnp.where(probed > 0.0, 0.0, NEG_FILL), (tile, LANES))
        raw = lax.dot_general(
            adapted, rows_ref[j], (((1,), (1,)), ((), ())), preferred_element_type=jnp.float32
        )
        for b in range(per // LANES):
            dead = jnp.where(live[j] > b * LANES, 0.0, NEG_FILL)
            piece = raw[:, b * LANES : (b + 1) * LANES] + (bias + dead)
            s_ref[:, j * per + b * LANES : j * per + (b + 1) * LANES] = piece
            top = jnp.maximum(top, piece)
    peak = jnp.max(top, axis=1, keepdims=True)
    peak_lanes = jnp.broadcast_to(peak, (tile, LANES))
    total = jnp.zeros((tile, LANES), jnp.float32)
    for b in range(lists * per // LANES):
        at = slice(b * LANES, (b + 1) * LANES)
        weight = jnp.exp((s_ref[:, at] - peak_lanes) * scale)
        total = total + weight
        p_ref[:, at] = weight.astype(jnp.bfloat16)
    stats_ref[0:1, :] = jnp.max(top.T, axis=0, keepdims=True)
    stats_ref[1:2, :] = jnp.sum(total.T, axis=0, keepdims=True)


def grad_kernel(place, local_ref, whole_ref, info_ref, p_ref, rows_ref, out_ref, g_ref):
    width = rows_ref.shape[1]
    scale = 1.0 / math.sqrt(width)
    tile = p_ref.shape[0]
    keys = p_ref.shape[1]
    factor = jnp.exp((local_ref[0:1, :] - whole_ref[0:1, :]) * scale) / whole_ref[1:2, :]
    factor = jnp.broadcast_to(factor, (LANES, tile)).T
    lane = lax.broadcasted_iota(jnp.int32, (tile, LANES), 1)
    info = info_ref[...].astype(jnp.float32)

    def column(n):
        return jnp.sum(jnp.where(lane == n, info, 0.0), axis=1, keepdims=True)

    slot = column(16) - place[4].astype(jnp.float32)
    row = column(17) * 64.0 + column(18) - place[5].astype(jnp.float32)
    per = 512.0
    inside = (slot >= 0.0) & (slot < keys / per) & (row >= 0.0) & (row < per)
    target = jnp.where(inside, slot * per + row, -1.0).astype(jnp.int32)
    target = jnp.broadcast_to(target, (tile, LANES))
    for b in range(keys // LANES):
        at = slice(b * LANES, (b + 1) * LANES)
        grad = p_ref[:, at].astype(jnp.float32) * factor - jnp.where(target == lane + b * LANES, 1.0, 0.0)
        g_ref[:, at] = grad.astype(jnp.bfloat16)
    out = jnp.dot(g_ref[...], rows_ref[...], preferred_element_type=jnp.float32) * scale
    out_ref[...] = out.astype(out_ref.dtype)


def adapter_kernel(place, q_ref, b_ref, out_ref, own):
    count = q_ref.shape[0]

    @pl.when(pl.program_id(0) == 0)
    def _():
        for i in range(8):
            base = tile_of(jnp.int32(i), place) * 256
            reorder_tile(
                b_ref.at[pl.ds(pl.multiple_of(base, 256), 256), :],
                own.at[i * 256 : (i + 1) * 256, :],
                place,
                own.shape[1],
            )

    out_ref[...] = lax.dot_general(
        q_ref[...], own[...], (((0,), (0,)), ((), ())), preferred_element_type=jnp.float32
    ) * (1.0 / math.sqrt(count))


def merge_stats(a, b, scale):
    top = jnp.maximum(a[0], b[0])
    total = a[1] * jnp.exp((a[0] - top) * scale) + b[1] * jnp.exp((b[0] - top) * scale)
    return jnp.stack([top, total])


def merge_axis(stats, axis, scale):
    parts = [stats] + [from_ahead(stats, axis, j) for j in range(1, lax.axis_size(axis))]
    top = functools.reduce(jnp.maximum, [p[0] for p in parts])
    total = sum(p[1] * jnp.exp((p[0] - top) * scale) for p in parts)
    return jnp.stack([top, total])


def on_device(queries, adapter_w, index_rows, probes, list_slot, block_counts, target_raw):
    width = queries.shape[1]
    scale = 1.0 / math.sqrt(width)
    lists_here, rows_here = index_rows.shape[0], index_rows.shape[1]
    place_z, place_c = lax.axis_index("z"), lax.axis_index("core")
    place_y, place_x = lax.axis_index("y"), lax.axis_index("x")
    first_slot = (place_z * 2 + place_c) * lists_here
    first_row = (place_y * 4 + place_x) * rows_here
    list_length = rows_here * 16
    place = jnp.stack([place_z, place_c, place_y, place_x, first_slot, first_row]).astype(jnp.int32)

    which = target_raw // list_length
    target_list = jnp.sum(
        jnp.where(jnp.arange(probes.shape[1], dtype=jnp.int32)[None, :] == which[:, None], probes, 0), axis=1
    )
    target_row = target_raw % list_length % (ROWS * table_lookup(block_counts, target_list))
    info = jnp.concatenate(
        [
            table_lookup(list_slot, probes),
            table_lookup(list_slot, target_list)[:, None],
            (target_row // 64)[:, None],
            (target_row % 64)[:, None],
            jnp.zeros((queries.shape[0], LANES - 19), jnp.int32),
        ],
        axis=1,
    ).astype(jnp.bfloat16)
    packed = gather_all(jnp.concatenate([queries, info], axis=1))
    count = packed.shape[0]

    slots_here = first_slot + jnp.arange(lists_here, dtype=jnp.int32)
    live = ROWS * jnp.sum(
        jnp.where(list_slot[None, :] == slots_here[:, None], block_counts[None, :], 0), axis=1
    ) - first_row

    tile = 256
    keys = lists_here * rows_here
    steps = count // tile
    whole = pl.BlockSpec(memory_space=pltpu.VMEM)
    q_all, info_all, weights, stats = pl.pallas_call(
        score_kernel,
        grid_spec=pltpu.PrefetchScalarGridSpec(
            num_scalar_prefetch=2,
            grid=(steps,),
            in_specs=[
                pl.BlockSpec((tile, width + LANES), lambda i, place, live: (tile_of(i, place), 0)),
                whole,
                whole,
            ],
            out_specs=[
                pl.BlockSpec((tile, width), lambda i, place, live: (i, 0)),
                pl.BlockSpec((tile, LANES), lambda i, place, live: (i, 0)),
                pl.BlockSpec((tile, keys), lambda i, place, live: (i, 0)),
                pl.BlockSpec((2, tile), lambda i, place, live: (0, i)),
            ],
            scratch_shapes=[
                pltpu.VMEM((tile, width + LANES), jnp.bfloat16),
                pltpu.VMEM((tile, keys), jnp.float32),
            ],
        ),
        out_shape=[
            jax.ShapeDtypeStruct((count, width), jnp.bfloat16),
            jax.ShapeDtypeStruct((count, LANES), jnp.bfloat16),
            jax.ShapeDtypeStruct((count, keys), jnp.bfloat16),
            jax.ShapeDtypeStruct((2, count), jnp.float32),
        ],
        compiler_params=pltpu.CompilerParams(vmem_limit_bytes=48 << 20),
        cost_estimate=pl.CostEstimate(
            flops=2 * count * width * (keys + width), bytes_accessed=count * keys * 2, transcendentals=count * keys
        ),
        name="scores",
    )(place, live.astype(jnp.int32), packed, adapter_w, index_rows)

    whole_stats = stats
    for axis in ("core", "x", "y", "z"):
        whole_stats = merge_axis(whole_stats, axis, scale)

    back_partial = pl.pallas_call(
        grad_kernel,
        grid_spec=pltpu.PrefetchScalarGridSpec(
            num_scalar_prefetch=1,
            grid=(steps,),
            in_specs=[
                pl.BlockSpec((2, tile), lambda i, place: (0, i)),
                pl.BlockSpec((2, tile), lambda i, place: (0, i)),
                pl.BlockSpec((tile, LANES), lambda i, place: (i, 0)),
                pl.BlockSpec((tile, keys), lambda i, place: (i, 0)),
                whole,
            ],
            out_specs=pl.BlockSpec((tile, width), lambda i, place: (i, 0)),
            scratch_shapes=[pltpu.VMEM((tile, keys), jnp.bfloat16)],
        ),
        out_shape=jax.ShapeDtypeStruct((count, width), jnp.bfloat16),
        compiler_params=pltpu.CompilerParams(vmem_limit_bytes=48 << 20),
        cost_estimate=pl.CostEstimate(
            flops=2 * count * width * keys, bytes_accessed=count * keys * 2, transcendentals=0
        ),
        name="grads",
    )(place, stats, whole_stats, info_all, weights, index_rows.reshape(keys, width))

    pieces = lax.all_to_all(back_partial, AXES, split_axis=0, concat_axis=0, tiled=True)
    back = jnp.sum(pieces.reshape(-1, queries.shape[0], width).astype(jnp.float32), axis=0)
    back_low = back.astype(jnp.bfloat16)
    query_grad = (
        back
        + lax.dot_general(back_low, adapter_w, (((1,), (1,)), ((), ())), preferred_element_type=jnp.float32)
    ).astype(jnp.bfloat16)
    all_back = gather_all(back_low)
    adapter_grad = pl.pallas_call(
        adapter_kernel,
        grid_spec=pltpu.PrefetchScalarGridSpec(
            num_scalar_prefetch=1,
            grid=(3,),
            in_specs=[
                pl.BlockSpec((count, width // 3), lambda i, place: (0, i)),
                whole,
            ],
            out_specs=pl.BlockSpec((width // 3, width), lambda i, place: (i, 0)),
            scratch_shapes=[pltpu.VMEM((count, width), jnp.bfloat16)],
        ),
        out_shape=jax.ShapeDtypeStruct((width, width), jnp.float32),
        compiler_params=pltpu.CompilerParams(vmem_limit_bytes=32 << 20),
        cost_estimate=pl.CostEstimate(flops=2 * count * width * width, bytes_accessed=count * width * 4, transcendentals=0),
        name="adapter",
    )(place, q_all, all_back)
    return (query_grad, adapter_grad)


def solution(mesh):
    split = Mesh(mesh.devices.reshape(SIZES), AXES)
    placed = (
        P(AXES, None),
        P(),
        P(("z", "core"), ("y", "x"), None),
        P(AXES, None),
        P(),
        P(),
        P(AXES),
    )
    return jax.shard_map(
        on_device,
        mesh=split,
        in_specs=placed,
        out_specs=(P(AXES, None), P()),
        check_vma=False,
    )
```

```python
import functools
import math

import jax
import jax.numpy as jnp
from jax import lax
from jax.experimental import pallas as pl
from jax.experimental.pallas import tpu as pltpu
from jax.sharding import Mesh
from jax.sharding import PartitionSpec as P

ROWS = 128
NEG_FILL = -1e30
LANES = 128
PROBES = 16
SIZES = (4, 2, 4, 4)
AXES = ("z", "core", "y", "x")
CHIPS = ("z", "y", "x")
LOG2E = 1.4426950408889634
WHOLE = pl.BlockSpec(memory_space=pltpu.VMEM)


def table_lookup(small_table, lookup_keys):
    matches = lookup_keys[..., None] == jnp.arange(small_table.shape[0], dtype=jnp.int32)
    return jnp.sum(jnp.where(matches, small_table, 0), axis=-1)


def from_ahead(value, axis, step):
    size = lax.axis_size(axis)
    return lax.ppermute(value, axis, [((i + step) % size, i) for i in range(size)])


def gather_pair(value):
    chips = lax.axis_size(CHIPS)
    spread = jnp.broadcast_to(value[None], (chips,) + value.shape).reshape((-1,) + value.shape[1:])
    own = lax.all_to_all(spread, CHIPS, split_axis=0, concat_axis=0, tiled=True)
    return own, from_ahead(own, "core", 1)


def lanes_of(column, tile):
    return jnp.broadcast_to(column, (tile, LANES))


def score_kernel(place, live, own_ref, other_ref, w_ref, rows_ref, p_ref, tops_ref, stats_ref, code_ref, q_ref, bias_ref, s_ref):
    width = w_ref.shape[0]
    half = own_ref.shape[0]
    tile = 2 * half
    lists, per = rows_ref.shape[0], rows_ref.shape[1]
    factor = LOG2E / math.sqrt(width)
    mine = pl.multiple_of(place[1] * half, half)
    theirs = pl.multiple_of((1 - place[1]) * half, half)
    q_ref[pl.ds(mine, half), :] = own_ref[...]
    q_ref[pl.ds(theirs, half), :] = other_ref[...]
    queries = q_ref[:, :width]
    info = q_ref[:, width:].astype(jnp.float32)
    adapted = (
        queries.astype(jnp.float32) + jnp.dot(queries, w_ref[...], preferred_element_type=jnp.float32)
    ).astype(jnp.bfloat16)
    lane = lax.broadcasted_iota(jnp.int32, (tile, LANES), 1)
    slots = jnp.where(lane < PROBES, info, -1.0)
    bias_ref[lists] = jnp.full((tile, LANES), NEG_FILL, jnp.float32)
    for j in range(lists):
        slot = (place[2] + j).astype(jnp.float32)
        probed = jnp.max(jnp.where(slots == slot, 1.0, 0.0), axis=1, keepdims=True)
        bias_ref[j] = lanes_of(jnp.where(probed > 0.0, 0.0, NEG_FILL), tile)

    def column(n):
        return jnp.sum(jnp.where(lane == n, info, 0.0), axis=1, keepdims=True)

    slot = column(PROBES) - place[2].astype(jnp.float32)
    row = column(PROBES + 1) * 64.0 + column(PROBES + 2) - place[3].astype(jnp.float32)
    inside = (slot >= 0.0) & (slot < float(lists)) & (row >= 0.0) & (row < float(per))
    code = lanes_of(jnp.where(inside, slot * float(per) + row, -1.0), tile)
    code_ref[...] = code.T[0:1, :]

    blocks = per // LANES

    def matmul(j):
        raw = lax.dot_general(
            adapted, rows_ref[j], (((1,), (1,)), ((), ())), preferred_element_type=jnp.float32
        )
        top = None
        for b in range(blocks):
            which = jnp.where(live[j] > b * LANES, j, lists)
            piece = raw[:, b * LANES : (b + 1) * LANES] + bias_ref[which]
            s_ref[j % 2, :, b * LANES : (b + 1) * LANES] = piece
            top = piece if top is None else jnp.maximum(top, piece)
        return top

    def weigh(j, top):
        peak = lanes_of(jnp.max(top, axis=1, keepdims=True), tile) * factor
        total = None
        for b in range(blocks):
            weight = jnp.exp2(s_ref[j % 2, :, b * LANES : (b + 1) * LANES] * factor - peak)
            total = weight if total is None else total + weight
            at = j * per + b * LANES
            p_ref[:, at : at + LANES] = weight.astype(jnp.bfloat16)
        return peak, total

    tops = jnp.full((tile, LANES), NEG_FILL, jnp.float32)
    high = total = None
    waiting = matmul(0)
    for j in range(lists):
        following = matmul(j + 1) if j + 1 < lists else None
        peak, part = weigh(j, waiting)
        tops = jnp.where(lane == j, peak, tops)
        if high is None:
            high, total = peak, part
        else:
            raised = jnp.maximum(high, peak)
            total = total * jnp.exp2(high - raised) + part * jnp.exp2(peak - raised)
            high = raised
        waiting = following
    tops_ref[...] = tops
    stats_ref[0:1, :] = high.T[0:1, :]
    stats_ref[1:2, :] = jnp.sum(total.T, axis=0, keepdims=True)


def back_kernel(stats_ref, code_ref, tops_ref, p_ref, rows_ref, out_ref, target_ref, g_ref, row_ref):
    lists, per, width = rows_ref.shape
    tile = p_ref.shape[0]
    high = jnp.broadcast_to(stats_ref[0:1, :], (LANES, tile)).T
    lane = lax.broadcasted_iota(jnp.int32, (tile, LANES), 1)
    share = jnp.exp2(tops_ref[...] - high)
    acc = None
    for j in range(lists):
        part = lanes_of(jnp.max(jnp.where(lane == j, share, 0.0), axis=1, keepdims=True), tile)
        for b in range(per // LANES):
            at = j * per + b * LANES
            g_ref[:, at : at + LANES] = (p_ref[:, at : at + LANES].astype(jnp.float32) * part).astype(jnp.bfloat16)
        out = jnp.dot(g_ref[:, j * per : (j + 1) * per], rows_ref[j], preferred_element_type=jnp.float32)
        acc = out if acc is None else acc + out
    out_ref[...] = acc

    row_ref[...] = jnp.zeros_like(row_ref)
    code = code_ref[...]
    index = lax.broadcasted_iota(jnp.int32, (1, tile), 1).astype(jnp.float32)
    sub = lax.broadcasted_iota(jnp.int32, (16, width), 0)
    none = float(tile)

    def first_after(last):
        return jnp.min(jnp.where((code >= 0.0) & (index > last), index, none))

    def step(at):
        key = jnp.max(jnp.where(index == at, code, -1.0)).astype(jnp.int32)
        group = rows_ref[key // per, pl.ds(pl.multiple_of((key % per) // 16 * 16, 16), 16), :]
        row = jnp.sum(jnp.where(sub == key % 16, group.astype(jnp.float32), 0.0), axis=0, keepdims=True)
        row_ref[pl.ds(at.astype(jnp.int32), 1), :] = row
        return first_after(at)

    lax.while_loop(lambda at: at < none, step, first_after(-1.0))
    target_ref[...] = row_ref[...].astype(jnp.bfloat16)


def scale_kernel(place, local_ref, whole_ref, out_ref, target_ref, mine_ref, theirs_ref, r_ref):
    tile, width = out_ref.shape
    half = tile // 2
    share = jnp.exp2(local_ref[0:1, :] - whole_ref[0:1, :]) / whole_ref[1:2, :]
    share = jnp.broadcast_to(share, (LANES, tile)).T
    for b in range(width // LANES):
        at = slice(b * LANES, (b + 1) * LANES)
        r_ref[:, at] = (
            (out_ref[:, at] * share - target_ref[:, at].astype(jnp.float32)) * (1.0 / math.sqrt(width))
        ).astype(jnp.bfloat16)
    mine_ref[...] = r_ref[pl.ds(pl.multiple_of(place[1] * half, half), half), :]
    theirs_ref[...] = r_ref[pl.ds(pl.multiple_of((1 - place[1]) * half, half), half), :]


def adapter_kernel(place, q_own, q_other, b_own, b_other, out_ref):
    count = 2 * q_own.shape[0]

    def product(q_first, b_first, q_second, b_second):
        turned = (((0,), (0,)), ((), ()))
        total = lax.dot_general(q_first[...], b_first[...], turned, preferred_element_type=jnp.float32)
        total = total + lax.dot_general(q_second[...], b_second[...], turned, preferred_element_type=jnp.float32)
        out_ref[...] = total * (1.0 / math.sqrt(count))

    @pl.when(place[1] == 0)
    def _():
        product(q_own, b_own, q_other, b_other)

    @pl.when(place[1] == 1)
    def _():
        product(q_other, b_other, q_own, b_own)


def merge_axis(stats, axis):
    parts = [stats] + [from_ahead(stats, axis, j) for j in range(1, lax.axis_size(axis))]
    top = functools.reduce(jnp.maximum, [p[0] for p in parts])
    total = sum(p[1] * jnp.exp2(p[0] - top) for p in parts)
    return jnp.stack([top, total])


def on_device(queries, adapter_w, index_rows, probes, list_slot, block_counts, target_raw):
    width = queries.shape[1]
    lists_here, rows_here = index_rows.shape[0], index_rows.shape[1]
    place_z, place_c = lax.axis_index("z"), lax.axis_index("core")
    place_y, place_x = lax.axis_index("y"), lax.axis_index("x")
    first_slot = (place_z * 2 + place_c) * lists_here
    first_row = (place_y * 4 + place_x) * rows_here
    list_length = rows_here * 16
    place = jnp.stack([place_z, place_c, first_slot, first_row]).astype(jnp.int32)

    which = target_raw // list_length
    target_list = jnp.sum(
        jnp.where(jnp.arange(probes.shape[1], dtype=jnp.int32)[None, :] == which[:, None], probes, 0), axis=1
    )
    target_row = target_raw % list_length % (ROWS * table_lookup(block_counts, target_list))
    info = jnp.concatenate(
        [
            table_lookup(list_slot, probes),
            table_lookup(list_slot, target_list)[:, None],
            (target_row // 64)[:, None],
            (target_row % 64)[:, None],
            jnp.zeros((queries.shape[0], LANES - PROBES - 3), jnp.int32),
        ],
        axis=1,
    ).astype(jnp.bfloat16)
    own, other = gather_pair(jnp.concatenate([queries, info], axis=1))
    count = 2 * own.shape[0]

    slots_here = first_slot + jnp.arange(lists_here, dtype=jnp.int32)
    live = (
        ROWS * jnp.sum(jnp.where(list_slot[None, :] == slots_here[:, None], block_counts[None, :], 0), axis=1)
        - first_row
    ).astype(jnp.int32)

    tile = 512
    half = tile // 2
    keys = lists_here * rows_here
    steps = count // tile
    weights, tops, stats, code = pl.pallas_call(
        score_kernel,
        grid_spec=pltpu.PrefetchScalarGridSpec(
            num_scalar_prefetch=2,
            grid=(steps,),
            in_specs=[
                pl.BlockSpec((half, width + LANES), lambda i, place, live: (i, 0)),
                pl.BlockSpec((half, width + LANES), lambda i, place, live: (i, 0)),
                WHOLE,
                WHOLE,
            ],
            out_specs=[
                pl.BlockSpec((tile, keys), lambda i, place, live: (i, 0)),
                pl.BlockSpec((tile, LANES), lambda i, place, live: (i, 0)),
                pl.BlockSpec((2, tile), lambda i, place, live: (0, i)),
                pl.BlockSpec((1, tile), lambda i, place, live: (0, i)),
            ],
            scratch_shapes=[
                pltpu.VMEM((tile, width + LANES), jnp.bfloat16),
                pltpu.VMEM((lists_here + 1, tile, LANES), jnp.float32),
                pltpu.VMEM((2, tile, rows_here), jnp.float32),
            ],
        ),
        out_shape=[
            jax.ShapeDtypeStruct((count, keys), jnp.bfloat16),
            jax.ShapeDtypeStruct((count, LANES), jnp.float32),
            jax.ShapeDtypeStruct((2, count), jnp.float32),
            jax.ShapeDtypeStruct((1, count), jnp.float32),
        ],
        compiler_params=pltpu.CompilerParams(vmem_limit_bytes=40 << 20),
        cost_estimate=pl.CostEstimate(
            flops=2 * count * width * (keys + width), bytes_accessed=count * keys * 2, transcendentals=count * keys
        ),
        name="scores",
    )(place, live, own, other, adapter_w, index_rows)

    backs = []
    for i in range(steps):
        backs.append(
            pl.pallas_call(
                back_kernel,
                grid=(1,),
                in_specs=[
                    pl.BlockSpec((2, tile), lambda k, i=i: (0, i)),
                    pl.BlockSpec((1, tile), lambda k, i=i: (0, i)),
                    pl.BlockSpec((tile, LANES), lambda k, i=i: (i, 0)),
                    pl.BlockSpec((tile, keys), lambda k, i=i: (i, 0)),
                    WHOLE,
                ],
                out_specs=[
                    pl.BlockSpec((tile, width), lambda k: (0, 0)),
                    pl.BlockSpec((tile, width), lambda k: (0, 0)),
                ],
                out_shape=[
                    jax.ShapeDtypeStruct((tile, width), jnp.float32),
                    jax.ShapeDtypeStruct((tile, width), jnp.bfloat16),
                ],
                scratch_shapes=[
                    pltpu.VMEM((tile, keys), jnp.bfloat16),
                    pltpu.VMEM((tile, width), jnp.float32),
                ],
                compiler_params=pltpu.CompilerParams(vmem_limit_bytes=40 << 20),
                cost_estimate=pl.CostEstimate(
                    flops=2 * tile * width * keys, bytes_accessed=tile * keys * 2, transcendentals=0
                ),
                name="backs",
            )(stats, code, tops, weights, index_rows)
        )

    whole_stats = stats
    for axis in ("core", "x", "y", "z"):
        whole_stats = merge_axis(whole_stats, axis)

    mine, theirs = [], []
    for i in range(steps):
        a, b = pl.pallas_call(
            scale_kernel,
            grid_spec=pltpu.PrefetchScalarGridSpec(
                num_scalar_prefetch=1,
                grid=(1,),
                in_specs=[
                    pl.BlockSpec((2, tile), lambda k, place, i=i: (0, i)),
                    pl.BlockSpec((2, tile), lambda k, place, i=i: (0, i)),
                    WHOLE,
                    WHOLE,
                ],
                out_specs=[WHOLE, WHOLE],
                scratch_shapes=[pltpu.VMEM((tile, width), jnp.bfloat16)],
            ),
            out_shape=[jax.ShapeDtypeStruct((half, width), jnp.bfloat16)] * 2,
            name="scaled",
        )(place, stats, whole_stats, *backs[i])
        mine.append(a)
        theirs.append(b)
    received = from_ahead(jnp.concatenate(theirs, axis=0), "core", 1)
    merged = (jnp.concatenate(mine, axis=0).astype(jnp.float32) + received.astype(jnp.float32)).astype(jnp.bfloat16)
    pieces = lax.all_to_all(merged, CHIPS, split_axis=0, concat_axis=0, tiled=True)
    back = jnp.sum(pieces.reshape(-1, queries.shape[0], width).astype(jnp.float32), axis=0)
    back_low = back.astype(jnp.bfloat16)
    query_grad = (
        back
        + lax.dot_general(back_low, adapter_w, (((1,), (1,)), ((), ())), preferred_element_type=jnp.float32)
    ).astype(jnp.bfloat16)
    b_own, b_other = gather_pair(back_low)
    third = width // 3
    adapter_grad = pl.pallas_call(
        adapter_kernel,
        grid_spec=pltpu.PrefetchScalarGridSpec(
            num_scalar_prefetch=1,
            grid=(3,),
            in_specs=[
                pl.BlockSpec((count // 2, third), lambda i, place: (0, i)),
                pl.BlockSpec((count // 2, third), lambda i, place: (0, i)),
                WHOLE,
                WHOLE,
            ],
            out_specs=pl.BlockSpec((third, width), lambda i, place: (i, 0)),
        ),
        out_shape=jax.ShapeDtypeStruct((width, width), jnp.float32),
        compiler_params=pltpu.CompilerParams(vmem_limit_bytes=24 << 20),
        cost_estimate=pl.CostEstimate(
            flops=2 * count * width * width, bytes_accessed=count * width * 4, transcendentals=0
        ),
        name="adapter",
    )(place, own, other, b_own, b_other)
    return (query_grad, adapter_grad)


def solution(mesh):
    split = Mesh(mesh.devices.reshape(SIZES), AXES)
    placed = (
        P(AXES, None),
        P(),
        P(("z", "core"), ("y", "x"), None),
        P(AXES, None),
        P(),
        P(),
        P(AXES),
    )
    return jax.shard_map(
        on_device,
        mesh=split,
        in_specs=placed,
        out_specs=(P(AXES, None), P()),
        check_vma=False,
    )
```

```python
import functools
import math

import jax
import jax.numpy as jnp
from jax import lax
from jax.experimental import pallas as pl
from jax.experimental.pallas import tpu as pltpu
from jax.sharding import Mesh
from jax.sharding import PartitionSpec as P

ROWS = 128
NEG_FILL = -1e30
LANES = 128
PROBES = 16
SIZES = (4, 2, 4, 4)
AXES = ("z", "core", "y", "x")
CHIPS = ("z", "y", "x")
LOG2E = 1.4426950408889634
WHOLE = pl.BlockSpec(memory_space=pltpu.VMEM)


def from_ahead(value, axis, step):
    size = lax.axis_size(axis)
    return lax.ppermute(value, axis, [((i + step) % size, i) for i in range(size)])


def spread_axes(value, axes):
    size = lax.axis_size(axes)
    spread = jnp.broadcast_to(value[None], (size,) + value.shape).reshape((-1,) + value.shape[1:])
    return lax.all_to_all(spread, axes, split_axis=0, concat_axis=0, tiled=True)


def lanes_of(column, tile):
    return jnp.broadcast_to(column, (tile, LANES))


def columns_of(rows, tile):
    return jnp.concatenate([rows, jnp.zeros((LANES - rows.shape[0], tile), jnp.float32)], axis=0).T


def score_kernel(
    place, list_slot, block_counts, own_ref, other_ref, w_ref, rows_ref,
    p_ref, tops_ref, stats_ref, code_ref, q_out, q_ref, bias_ref, s_ref, here_ref,
):
    width = w_ref.shape[0]
    tile = own_ref.shape[0]
    lists, per = rows_ref.shape[0], rows_ref.shape[1]
    factor = LOG2E / math.sqrt(width)
    core = pl.program_id(0)

    def find(n, _):
        at = list_slot[n] - place[2]
        here_ref[jnp.where((at >= 0) & (at < lists), at, lists)] = n
        return 0

    lax.fori_loop(0, list_slot.shape[0], find, 0)
    here = [here_ref[j] for j in range(lists)]
    total_rows = [ROWS * block_counts[n] for n in here]
    live = [n - place[3] for n in total_rows]

    @pl.when(core == place[1])
    def _():
        q_ref[...] = own_ref[...]

    @pl.when(core != place[1])
    def _():
        q_ref[...] = other_ref[...]

    queries = q_ref[:, :width]
    q_out[...] = queries
    adapted = (
        queries.astype(jnp.float32) + jnp.dot(queries, w_ref[...], preferred_element_type=jnp.float32)
    ).astype(jnp.bfloat16)

    info = q_ref[:, width:].astype(jnp.float32).T
    probes = info[0:PROBES, :]
    number = lax.broadcasted_iota(jnp.int32, (PROBES, tile), 0).astype(jnp.float32)
    target = jnp.sum(jnp.where(number == info[PROBES : PROBES + 1, :], probes, 0.0), axis=0, keepdims=True)
    raw_row = info[PROBES + 1 : PROBES + 2, :] * 64.0 + info[PROBES + 2 : PROBES + 3, :]
    code = jnp.full((1, tile), -1.0, jnp.float32)
    bias = []
    for j in range(lists):
        name = here[j].astype(jnp.float32)
        probed = jnp.max(jnp.where(probes == name, 1.0, 0.0), axis=0, keepdims=True)
        bias.append(jnp.where(probed > 0.0, 0.0, NEG_FILL))
        length = total_rows[j].astype(jnp.float32)
        row = raw_row - jnp.where(raw_row >= length, length, 0.0) - place[3].astype(jnp.float32)
        inside = (target == name) & (row >= 0.0) & (row < float(per))
        code = jnp.where(inside, row + float(j * per), code)
    code_ref[...] = code
    bias = columns_of(jnp.concatenate(bias, axis=0), tile)
    for j in range(lists):
        bias_ref[j] = lanes_of(bias[:, j : j + 1], tile)
    bias_ref[lists] = jnp.full((tile, LANES), NEG_FILL, jnp.float32)

    lane = lax.broadcasted_iota(jnp.int32, (tile, LANES), 1)
    blocks = per // LANES

    def matmul(j):
        raw = lax.dot_general(
            adapted, rows_ref[j], (((1,), (1,)), ((), ())), preferred_element_type=jnp.float32
        )
        top = None
        for b in range(blocks):
            which = jnp.where(live[j] > b * LANES, j, lists)
            piece = raw[:, b * LANES : (b + 1) * LANES] + bias_ref[which]
            s_ref[j % 2, :, b * LANES : (b + 1) * LANES] = piece
            top = piece if top is None else jnp.maximum(top, piece)
        return top

    def weigh(j, top):
        peak = lanes_of(jnp.max(top, axis=1, keepdims=True), tile) * factor
        total = None
        for b in range(blocks):
            weight = jnp.exp2(s_ref[j % 2, :, b * LANES : (b + 1) * LANES] * factor - peak)
            total = weight if total is None else total + weight
            at = j * per + b * LANES
            p_ref[:, at : at + LANES] = weight.astype(jnp.bfloat16)
        return peak, lanes_of(jnp.sum(total, axis=1, keepdims=True), tile)

    tops = jnp.full((tile, LANES), NEG_FILL, jnp.float32)
    sums = jnp.zeros((tile, LANES), jnp.float32)
    waiting = matmul(0)
    for j in range(lists):
        following = matmul(j + 1) if j + 1 < lists else None
        peak, total = weigh(j, waiting)
        tops = jnp.where(lane == j, peak, tops)
        sums = jnp.where(lane == j, total, sums)
        waiting = following
    tops = tops.T[0:lists, :]
    sums = sums.T[0:lists, :]
    tops_ref[...] = tops
    high = jnp.max(tops, axis=0, keepdims=True)
    stats_ref[0:1, :] = high
    stats_ref[1:2, :] = jnp.sum(sums * jnp.exp2(tops - high), axis=0, keepdims=True)


def back_kernel(stats_ref, code_ref, tops_ref, p_ref, rows_ref, *refs):
    out_ref, target_ref, g_ref, row_ref = refs[-4:]
    lists, per, width = rows_ref.shape
    tile = p_ref.shape[0]
    share = columns_of(jnp.exp2(tops_ref[...] - stats_ref[0:1, :]), tile)
    acc = None
    for j in range(lists):
        part = lanes_of(share[:, j : j + 1], tile)
        for b in range(per // LANES):
            at = j * per + b * LANES
            g_ref[:, at : at + LANES] = (p_ref[:, at : at + LANES].astype(jnp.float32) * part).astype(jnp.bfloat16)
        out = jnp.dot(g_ref[:, j * per : (j + 1) * per], rows_ref[j], preferred_element_type=jnp.float32)
        acc = out if acc is None else acc + out
    out_ref[...] = acc

    row_ref[...] = jnp.zeros_like(row_ref)
    code = code_ref[...]
    index = lax.broadcasted_iota(jnp.int32, (1, tile), 1).astype(jnp.float32)
    sub = lax.broadcasted_iota(jnp.int32, (16, width), 0)
    none = float(tile)

    def first_after(last):
        return jnp.min(jnp.where((code >= 0.0) & (index > last), index, none))

    def step(at):
        key = jnp.max(jnp.where(index == at, code, -1.0)).astype(jnp.int32)
        group = rows_ref[key // per, pl.ds(pl.multiple_of((key % per) // 16 * 16, 16), 16), :]
        row = jnp.sum(jnp.where(sub == key % 16, group.astype(jnp.float32), 0.0), axis=0, keepdims=True)
        row_ref[pl.ds(at.astype(jnp.int32), 1), :] = row
        return first_after(at)

    lax.while_loop(lambda at: at < none, step, first_after(-1.0))
    target_ref[...] = row_ref[...].astype(jnp.bfloat16)


def scale_kernel(place, local_ref, whole_ref, out_ref, target_ref, mine_ref, theirs_ref, r_ref):
    tile, width = out_ref.shape
    half = tile // 2
    share = jnp.exp2(local_ref[0:1, :] - whole_ref[0:1, :]) / whole_ref[1:2, :]
    share = jnp.broadcast_to(share, (LANES, tile)).T
    for b in range(width // LANES):
        at = slice(b * LANES, (b + 1) * LANES)
        r_ref[:, at] = (
            (out_ref[:, at] * share - target_ref[:, at].astype(jnp.float32)) * (1.0 / math.sqrt(width))
        ).astype(jnp.bfloat16)
    mine_ref[...] = r_ref[pl.ds(pl.multiple_of(place[1] * half, half), half), :]
    theirs_ref[...] = r_ref[pl.ds(pl.multiple_of((1 - place[1]) * half, half), half), :]


def adapter_kernel(place, q0, q1, q2, q3, b_own, b_other, out_ref, q_ref, b_ref):
    tile = q0.shape[0]
    half = tile // 2
    count = 4 * tile

    @pl.when(pl.program_id(0) == 0)
    def _():
        for i in range(4):
            for source, core in ((b_own, place[1]), (b_other, 1 - place[1])):
                to = pl.multiple_of(i * tile + core * half, half)
                b_ref[pl.ds(to, half), :] = source[i * half : (i + 1) * half, :]

    for i, q in enumerate((q0, q1, q2, q3)):
        to = pl.multiple_of(lax.rem(place[0] + i, 4) * tile, tile)
        q_ref[pl.ds(to, tile), :] = q[...]
    out_ref[...] = lax.dot_general(
        q_ref[...], b_ref[...], (((0,), (0,)), ((), ())), preferred_element_type=jnp.float32
    ) * (1.0 / math.sqrt(count))


def merge_axis(stats, axis):
    chunk = stats.shape[1] // 4
    parts = [stats]
    for j in range(1, lax.axis_size(axis)):
        part = from_ahead(stats, axis, j)
        if axis == "z":
            part = jnp.concatenate([part[:, (4 - j) * chunk :], part[:, : (4 - j) * chunk]], axis=1)
        parts.append(part)
    top = functools.reduce(jnp.maximum, [p[0] for p in parts])
    total = sum(p[1] * jnp.exp2(p[0] - top) for p in parts)
    return jnp.stack([top, total])


def on_device(queries, adapter_w, index_rows, probes, list_slot, block_counts, target_raw):
    width = queries.shape[1]
    lists_here, rows_here = index_rows.shape[0], index_rows.shape[1]
    place_z, place_c = lax.axis_index("z"), lax.axis_index("core")
    place_y, place_x = lax.axis_index("y"), lax.axis_index("x")
    first_slot = (place_z * 2 + place_c) * lists_here
    first_row = (place_y * 4 + place_x) * rows_here
    list_length = rows_here * 16
    place = jnp.stack([place_z, place_c, first_slot, first_row]).astype(jnp.int32)

    lane = jnp.arange(LANES, dtype=jnp.int32)[None, :]
    raw_row = lax.rem(target_raw, list_length)[:, None]
    info = jnp.pad(probes, ((0, 0), (0, LANES - PROBES)))
    info = jnp.where(lane == PROBES, lax.div(target_raw, list_length)[:, None], info)
    info = jnp.where(lane == PROBES + 1, lax.div(raw_row, 64), info)
    info = jnp.where(lane == PROBES + 2, lax.rem(raw_row, 64), info)
    plane = spread_axes(jnp.concatenate([queries, info.astype(jnp.bfloat16)], axis=1), ("y", "x"))

    half = plane.shape[0]
    tile = 2 * half
    steps = 4
    count = steps * tile
    keys = lists_here * rows_here
    owns = [plane] + [from_ahead(plane, "z", j) for j in range(1, steps)]
    weights, tops, stats, codes, gathered = [], [], [], [], []
    for own in owns:
        outs = pl.pallas_call(
            score_kernel,
            grid_spec=pltpu.PrefetchScalarGridSpec(
                num_scalar_prefetch=3,
                grid=(2,),
                in_specs=[WHOLE, WHOLE, WHOLE, WHOLE],
                out_specs=[
                    pl.BlockSpec((half, keys), lambda i, *_: (i, 0)),
                    pl.BlockSpec((lists_here, half), lambda i, *_: (0, i)),
                    pl.BlockSpec((2, half), lambda i, *_: (0, i)),
                    pl.BlockSpec((1, half), lambda i, *_: (0, i)),
                    pl.BlockSpec((half, width), lambda i, *_: (i, 0)),
                ],
                scratch_shapes=[
                    pltpu.VMEM((half, width + LANES), jnp.bfloat16),
                    pltpu.VMEM((lists_here + 1, half, LANES), jnp.float32),
                    pltpu.VMEM((2, half, rows_here), jnp.float32),
                    pltpu.SMEM((lists_here + 1,), jnp.int32),
                ],
            ),
            out_shape=[
                jax.ShapeDtypeStruct((tile, keys), jnp.bfloat16),
                jax.ShapeDtypeStruct((lists_here, tile), jnp.float32),
                jax.ShapeDtypeStruct((2, tile), jnp.float32),
                jax.ShapeDtypeStruct((1, tile), jnp.float32),
                jax.ShapeDtypeStruct((tile, width), jnp.bfloat16),
            ],
            compiler_params=pltpu.CompilerParams(vmem_limit_bytes=24 << 20),
            cost_estimate=pl.CostEstimate(
                flops=2 * tile * width * (keys + width), bytes_accessed=tile * keys * 2, transcendentals=tile * keys
            ),
            name="scores",
        )(place, list_slot, block_counts, own, from_ahead(own, "core", 1), adapter_w, index_rows)
        for kept, value in zip((weights, tops, stats, codes, gathered), outs):
            kept.append(value)

    out_all = target_all = None
    for i in range(steps):
        rest = [] if i == 0 else [out_all, target_all]
        out_all, target_all = pl.pallas_call(
            back_kernel,
            grid=(2,),
            in_specs=[
                pl.BlockSpec((2, half), lambda k: (0, k)),
                pl.BlockSpec((1, half), lambda k: (0, k)),
                pl.BlockSpec((lists_here, half), lambda k: (0, k)),
                pl.BlockSpec((half, keys), lambda k: (k, 0)),
                WHOLE,
            ]
            + [pl.BlockSpec(memory_space=pl.ANY)] * len(rest),
            out_specs=[pl.BlockSpec((half, width), lambda k, i=i: (2 * i + k, 0))] * 2,
            out_shape=[
                jax.ShapeDtypeStruct((count, width), jnp.float32),
                jax.ShapeDtypeStruct((count, width), jnp.bfloat16),
            ],
            scratch_shapes=[
                pltpu.VMEM((half, keys), jnp.bfloat16),
                pltpu.VMEM((half, width), jnp.float32),
            ],
            input_output_aliases={5: 0, 6: 1} if rest else {},
            compiler_params=pltpu.CompilerParams(vmem_limit_bytes=24 << 20),
            cost_estimate=pl.CostEstimate(
                flops=2 * tile * width * keys, bytes_accessed=tile * keys * 2, transcendentals=0
            ),
            name="backs",
        )(stats[i], codes[i], tops[i], weights[i], index_rows, *rest)

    local_stats = jnp.concatenate(stats, axis=1)
    whole_stats = local_stats
    for axis in ("core", "x", "y", "z"):
        whole_stats = merge_axis(whole_stats, axis)

    placed = pl.BlockSpec((half, width), lambda i, place: (lax.rem(place[0] + i, 4), 0))
    mine, theirs = pl.pallas_call(
        scale_kernel,
        grid_spec=pltpu.PrefetchScalarGridSpec(
            num_scalar_prefetch=1,
            grid=(steps,),
            in_specs=[
                pl.BlockSpec((2, tile), lambda i, place: (0, i)),
                pl.BlockSpec((2, tile), lambda i, place: (0, i)),
                pl.BlockSpec((tile, width), lambda i, place: (i, 0)),
                pl.BlockSpec((tile, width), lambda i, place: (i, 0)),
            ],
            out_specs=[placed, placed],
            scratch_shapes=[pltpu.VMEM((tile, width), jnp.bfloat16)],
        ),
        out_shape=[jax.ShapeDtypeStruct((count // 2, width), jnp.bfloat16)] * 2,
        compiler_params=pltpu.CompilerParams(vmem_limit_bytes=24 << 20),
        name="scaled",
    )(place, local_stats, whole_stats, out_all, target_all)
    received = from_ahead(theirs, "core", 1)
    merged = (mine.astype(jnp.float32) + received.astype(jnp.float32)).astype(jnp.bfloat16)
    pieces = lax.all_to_all(merged, CHIPS, split_axis=0, concat_axis=0, tiled=True)
    back = jnp.sum(pieces.reshape(-1, queries.shape[0], width).astype(jnp.float32), axis=0)
    back_low = back.astype(jnp.bfloat16)
    query_grad = (
        back
        + lax.dot_general(back_low, adapter_w, (((1,), (1,)), ((), ())), preferred_element_type=jnp.float32)
    ).astype(jnp.bfloat16)
    b_own = spread_axes(back_low, CHIPS)
    b_other = from_ahead(b_own, "core", 1)
    third = width // 3
    column = pl.BlockSpec((tile, third), lambda i, place: (0, i))
    adapter_grad = pl.pallas_call(
        adapter_kernel,
        grid_spec=pltpu.PrefetchScalarGridSpec(
            num_scalar_prefetch=1,
            grid=(3,),
            in_specs=[column, column, column, column, WHOLE, WHOLE],
            out_specs=pl.BlockSpec((third, width), lambda i, place: (i, 0)),
            scratch_shapes=[
                pltpu.VMEM((count, third), jnp.bfloat16),
                pltpu.VMEM((count, width), jnp.bfloat16),
            ],
        ),
        out_shape=jax.ShapeDtypeStruct((width, width), jnp.float32),
        compiler_params=pltpu.CompilerParams(vmem_limit_bytes=24 << 20),
        cost_estimate=pl.CostEstimate(
            flops=2 * count * width * width, bytes_accessed=count * width * 4, transcendentals=0
        ),
        name="adapter",
    )(place, *gathered, b_own, b_other)
    return (query_grad, adapter_grad)


def solution(mesh):
    split = Mesh(mesh.devices.reshape(SIZES), AXES)
    placed = (
        P(AXES, None),
        P(),
        P(("z", "core"), ("y", "x"), None),
        P(AXES, None),
        P(),
        P(),
        P(AXES),
    )
    return jax.shard_map(
        on_device,
        mesh=split,
        in_specs=placed,
        out_specs=(P(AXES, None), P()),
        check_vma=False,
    )
```

```python
import functools
import math

import jax
import jax.numpy as jnp
from jax import lax
from jax.experimental import pallas as pl
from jax.experimental.pallas import tpu as pltpu
from jax.sharding import Mesh
from jax.sharding import PartitionSpec as P

ROWS = 128
NEG_FILL = -1e30
LANES = 128
PROBES = 16
SIZES = (4, 2, 4, 4)
AXES = ("z", "core", "y", "x")
CHIPS = ("z", "y", "x")
ORDER = (0, 1, 3, 2)
LOG2E = 1.4426950408889634
WHOLE = pl.BlockSpec(memory_space=pltpu.VMEM)


def from_ahead(value, axis, step):
    size = lax.axis_size(axis)
    return lax.ppermute(value, axis, [((i + step) % size, i) for i in range(size)])


def chunk_of(i):
    return jnp.where(i < 2, i, 5 - i)


def spread_axes(value, axes):
    size = lax.axis_size(axes)
    spread = jnp.broadcast_to(value[None], (size,) + value.shape).reshape((-1,) + value.shape[1:])
    return lax.all_to_all(spread, axes, split_axis=0, concat_axis=0, tiled=True)


def lanes_of(column, tile):
    return jnp.broadcast_to(column, (tile, LANES))


def columns_of(rows, tile):
    return jnp.concatenate([rows, jnp.zeros((LANES - rows.shape[0], tile), jnp.float32)], axis=0).T


def score_kernel(
    place, list_slot, block_counts, own_ref, other_ref, w_ref, rows_ref,
    p_ref, tops_ref, stats_ref, code_ref, q_out, q_ref, bias_ref, s_ref, here_ref,
):
    width = w_ref.shape[0]
    tile = own_ref.shape[0]
    lists, per = rows_ref.shape[0], rows_ref.shape[1]
    factor = LOG2E / math.sqrt(width)
    core = pl.program_id(0)

    def find(n, _):
        at = list_slot[n] - place[2]
        here_ref[jnp.where((at >= 0) & (at < lists), at, lists)] = n
        return 0

    lax.fori_loop(0, list_slot.shape[0], find, 0)
    here = [here_ref[j] for j in range(lists)]
    total_rows = [ROWS * block_counts[n] for n in here]
    live = [n - place[3] for n in total_rows]

    @pl.when(core == place[1])
    def _():
        q_ref[...] = own_ref[...]

    @pl.when(core != place[1])
    def _():
        q_ref[...] = other_ref[...]

    queries = q_ref[:, :width]
    q_out[...] = queries
    adapted = (
        queries.astype(jnp.float32) + jnp.dot(queries, w_ref[...], preferred_element_type=jnp.float32)
    ).astype(jnp.bfloat16)

    info = q_ref[:, width:].astype(jnp.float32).T
    probes = info[0:PROBES, :]
    number = lax.broadcasted_iota(jnp.int32, (PROBES, tile), 0).astype(jnp.float32)
    target = jnp.sum(jnp.where(number == info[PROBES : PROBES + 1, :], probes, 0.0), axis=0, keepdims=True)
    raw_row = info[PROBES + 1 : PROBES + 2, :] * 64.0 + info[PROBES + 2 : PROBES + 3, :]
    code = jnp.full((1, tile), -1.0, jnp.float32)
    bias = []
    for j in range(lists):
        name = here[j].astype(jnp.float32)
        probed = jnp.max(jnp.where(probes == name, 1.0, 0.0), axis=0, keepdims=True)
        bias.append(jnp.where(probed > 0.0, 0.0, NEG_FILL))
        length = total_rows[j].astype(jnp.float32)
        row = raw_row - jnp.where(raw_row >= length, length, 0.0) - place[3].astype(jnp.float32)
        inside = (target == name) & (row >= 0.0) & (row < float(per))
        code = jnp.where(inside, row + float(j * per), code)
    code_ref[...] = code
    bias = columns_of(jnp.concatenate(bias, axis=0), tile)
    for j in range(lists):
        bias_ref[j] = lanes_of(bias[:, j : j + 1], tile)
    bias_ref[lists] = jnp.full((tile, LANES), NEG_FILL, jnp.float32)

    lane = lax.broadcasted_iota(jnp.int32, (tile, LANES), 1)
    blocks = per // LANES

    def matmul(j):
        raw = lax.dot_general(
            adapted, rows_ref[j], (((1,), (1,)), ((), ())), preferred_element_type=jnp.float32
        )
        top = None
        for b in range(blocks):
            which = jnp.where(live[j] > b * LANES, j, lists)
            piece = raw[:, b * LANES : (b + 1) * LANES] + bias_ref[which]
            s_ref[j % 2, :, b * LANES : (b + 1) * LANES] = piece
            top = piece if top is None else jnp.maximum(top, piece)
        return top

    def weigh(j, top):
        peak = lanes_of(jnp.max(top, axis=1, keepdims=True), tile) * factor
        total = None
        for b in range(blocks):
            weight = jnp.exp2(s_ref[j % 2, :, b * LANES : (b + 1) * LANES] * factor - peak)
            total = weight if total is None else total + weight
            at = j * per + b * LANES
            p_ref[:, at : at + LANES] = weight.astype(jnp.bfloat16)
        return peak, lanes_of(jnp.sum(total, axis=1, keepdims=True), tile)

    tops = jnp.full((tile, LANES), NEG_FILL, jnp.float32)
    sums = jnp.zeros((tile, LANES), jnp.float32)
    waiting = matmul(0)
    for j in range(lists):
        following = matmul(j + 1) if j + 1 < lists else None
        peak, total = weigh(j, waiting)
        tops = jnp.where(lane == j, peak, tops)
        sums = jnp.where(lane == j, total, sums)
        waiting = following
    tops = tops.T[0:lists, :]
    sums = sums.T[0:lists, :]
    tops_ref[...] = tops
    high = jnp.max(tops, axis=0, keepdims=True)
    stats_ref[0:1, :] = high
    stats_ref[1:2, :] = jnp.sum(sums * jnp.exp2(tops - high), axis=0, keepdims=True)


def back_kernel(stats_ref, code_ref, tops_ref, p_ref, rows_ref, *refs):
    out_ref, target_ref, g_ref, row_ref = refs[-4:]
    lists, per, width = rows_ref.shape
    tile = p_ref.shape[0]
    share = columns_of(jnp.exp2(tops_ref[...] - stats_ref[0:1, :]), tile)
    acc = None
    for j in range(lists):
        part = lanes_of(share[:, j : j + 1], tile)
        for b in range(per // LANES):
            at = j * per + b * LANES
            g_ref[:, at : at + LANES] = (p_ref[:, at : at + LANES].astype(jnp.float32) * part).astype(jnp.bfloat16)
        out = jnp.dot(g_ref[:, j * per : (j + 1) * per], rows_ref[j], preferred_element_type=jnp.float32)
        acc = out if acc is None else acc + out
    out_ref[...] = acc

    row_ref[...] = jnp.zeros_like(row_ref)
    code = code_ref[...]
    index = lax.broadcasted_iota(jnp.int32, (1, tile), 1).astype(jnp.float32)
    sub = lax.broadcasted_iota(jnp.int32, (16, width), 0)
    none = float(tile)

    def first_after(last):
        return jnp.min(jnp.where((code >= 0.0) & (index > last), index, none))

    def step(at):
        key = jnp.max(jnp.where(index == at, code, -1.0)).astype(jnp.int32)
        group = rows_ref[key // per, pl.ds(pl.multiple_of((key % per) // 16 * 16, 16), 16), :]
        row = jnp.sum(jnp.where(sub == key % 16, group.astype(jnp.float32), 0.0), axis=0, keepdims=True)
        row_ref[pl.ds(at.astype(jnp.int32), 1), :] = row
        return first_after(at)

    lax.while_loop(lambda at: at < none, step, first_after(-1.0))
    target_ref[...] = row_ref[...].astype(jnp.bfloat16)


def scale_kernel(place, local_ref, whole_ref, out_ref, target_ref, mine_ref, theirs_ref, r_ref):
    tile, width = out_ref.shape
    half = tile // 2
    share = jnp.exp2(local_ref[0:1, :] - whole_ref[0:1, :]) / whole_ref[1:2, :]
    share = jnp.broadcast_to(share, (LANES, tile)).T
    for b in range(width // LANES):
        at = slice(b * LANES, (b + 1) * LANES)
        r_ref[:, at] = (
            (out_ref[:, at] * share - target_ref[:, at].astype(jnp.float32)) * (1.0 / math.sqrt(width))
        ).astype(jnp.bfloat16)
    mine_ref[...] = r_ref[pl.ds(pl.multiple_of(place[1] * half, half), half), :]
    theirs_ref[...] = r_ref[pl.ds(pl.multiple_of((1 - place[1]) * half, half), half), :]


def adapter_kernel(place, q0, q1, q2, q3, b_own, b_other, out_ref, q_ref, b_ref):
    tile = q0.shape[0]
    half = tile // 2
    count = 4 * tile

    @pl.when(pl.program_id(0) == 0)
    def _():
        for i in range(4):
            for source, core in ((b_own, place[1]), (b_other, 1 - place[1])):
                to = pl.multiple_of(i * tile + core * half, half)
                b_ref[pl.ds(to, half), :] = source[i * half : (i + 1) * half, :]

    for ahead, q in zip(ORDER, (q0, q1, q2, q3)):
        to = pl.multiple_of(lax.rem(place[0] + ahead, 4) * tile, tile)
        q_ref[pl.ds(to, tile), :] = q[...]
    out_ref[...] = lax.dot_general(
        q_ref[...], b_ref[...], (((0,), (0,)), ((), ())), preferred_element_type=jnp.float32
    ) * (1.0 / math.sqrt(count))


def merge_axis(stats, axis):
    chunk = stats.shape[1] // 4
    parts = [stats]
    for j in range(1, lax.axis_size(axis)):
        part = from_ahead(stats, axis, j)
        if axis == "z":
            at = [ORDER.index((ahead - j) % 4) for ahead in ORDER]
            part = jnp.concatenate([part[:, k * chunk : (k + 1) * chunk] for k in at], axis=1)
        parts.append(part)
    top = functools.reduce(jnp.maximum, [p[0] for p in parts])
    total = sum(p[1] * jnp.exp2(p[0] - top) for p in parts)
    return jnp.stack([top, total])


def all_steps(queries, adapter_w, index_rows, probes, list_slot, block_counts, target_raw):
    width = queries.shape[1]
    lists_here, rows_here = index_rows.shape[0], index_rows.shape[1]
    place_z, place_c = lax.axis_index("z"), lax.axis_index("core")
    place_y, place_x = lax.axis_index("y"), lax.axis_index("x")
    first_slot = (place_z * 2 + place_c) * lists_here
    first_row = (place_y * 4 + place_x) * rows_here
    list_length = rows_here * 16
    place = jnp.stack([place_z, place_c, first_slot, first_row]).astype(jnp.int32)

    lane = jnp.arange(LANES, dtype=jnp.int32)[None, :]
    raw_row = lax.rem(target_raw, list_length)[:, None]
    info = jnp.pad(probes, ((0, 0), (0, LANES - PROBES)))
    info = jnp.where(lane == PROBES, lax.div(target_raw, list_length)[:, None], info)
    info = jnp.where(lane == PROBES + 1, lax.div(raw_row, 64), info)
    info = jnp.where(lane == PROBES + 2, lax.rem(raw_row, 64), info)
    plane = spread_axes(jnp.concatenate([queries, info.astype(jnp.bfloat16)], axis=1), ("y", "x"))

    half = plane.shape[0]
    tile = 2 * half
    steps = 4
    count = steps * tile
    keys = lists_here * rows_here
    owns = [plane]
    for ahead in ORDER[1:]:
        owns.append(from_ahead(plane, "z", ahead))
    weights, tops, stats, codes, gathered = [], [], [], [], []
    for ahead, own in zip(ORDER, owns):
        other = from_ahead(own, "core", 1)
        call = pl.pallas_call(
            score_kernel,
            grid_spec=pltpu.PrefetchScalarGridSpec(
                num_scalar_prefetch=3,
                grid=(2,),
                in_specs=[
                    pl.BlockSpec((half, width + LANES), lambda i, *_: (0, 0)),
                    pl.BlockSpec((half, width + LANES), lambda i, *_: (0, 0)),
                    WHOLE,
                    WHOLE,
                ],
                out_specs=[
                    pl.BlockSpec((half, keys), lambda i, *_: (i, 0)),
                    pl.BlockSpec((lists_here, half), lambda i, *_: (0, i)),
                    pl.BlockSpec((2, half), lambda i, *_: (0, i)),
                    pl.BlockSpec((1, half), lambda i, *_: (0, i)),
                    pl.BlockSpec((half, width), lambda i, *_: (i, 0)),
                ],
                scratch_shapes=[
                    pltpu.VMEM((half, width + LANES), jnp.bfloat16),
                    pltpu.VMEM((lists_here + 1, half, LANES), jnp.float32),
                    pltpu.VMEM((2, half, rows_here), jnp.float32),
                    pltpu.SMEM((lists_here + 1,), jnp.int32),
                ],
            ),
            out_shape=[
                jax.ShapeDtypeStruct((tile, keys), jnp.bfloat16),
                jax.ShapeDtypeStruct((lists_here, tile), jnp.float32),
                jax.ShapeDtypeStruct((2, tile), jnp.float32),
                jax.ShapeDtypeStruct((1, tile), jnp.float32),
                jax.ShapeDtypeStruct((tile, width), jnp.bfloat16),
            ],
            compiler_params=pltpu.CompilerParams(vmem_limit_bytes=24 << 20),
            cost_estimate=pl.CostEstimate(
                flops=2 * tile * width * (keys + width), bytes_accessed=tile * keys * 2, transcendentals=tile * keys
            ),
            name="scores",
        )
        outs = call(place, list_slot, block_counts, own, other, adapter_w, index_rows)
        for kept, value in zip((weights, tops, stats, codes, gathered), outs):
            kept.append(value)

    out_all = target_all = None
    for i in range(steps):
        rest = [] if i == 0 else [out_all, target_all]
        out_all, target_all = pl.pallas_call(
            back_kernel,
            grid=(2,),
            in_specs=[
                pl.BlockSpec((2, half), lambda k: (0, k)),
                pl.BlockSpec((1, half), lambda k: (0, k)),
                pl.BlockSpec((lists_here, half), lambda k: (0, k)),
                pl.BlockSpec((half, keys), lambda k: (k, 0)),
                WHOLE,
            ]
            + [pl.BlockSpec(memory_space=pl.ANY)] * len(rest),
            out_specs=[pl.BlockSpec((half, width), lambda k, i=i: (2 * i + k, 0))] * 2,
            out_shape=[
                jax.ShapeDtypeStruct((count, width), jnp.float32),
                jax.ShapeDtypeStruct((count, width), jnp.bfloat16),
            ],
            scratch_shapes=[
                pltpu.VMEM((half, keys), jnp.bfloat16),
                pltpu.VMEM((half, width), jnp.float32),
            ],
            input_output_aliases={5: 0, 6: 1} if rest else {},
            compiler_params=pltpu.CompilerParams(vmem_limit_bytes=24 << 20),
            cost_estimate=pl.CostEstimate(
                flops=2 * tile * width * keys, bytes_accessed=tile * keys * 2, transcendentals=0
            ),
            name="backs",
        )(stats[i], codes[i], tops[i], weights[i], index_rows, *rest)

    local_stats = jnp.concatenate(stats, axis=1)
    whole_stats = local_stats
    for axis in ("core", "x", "y", "z"):
        whole_stats = merge_axis(whole_stats, axis)

    placed = pl.BlockSpec((half, width), lambda i, place: (lax.rem(place[0] + chunk_of(i), 4), 0))
    mine, theirs = pl.pallas_call(
        scale_kernel,
        grid_spec=pltpu.PrefetchScalarGridSpec(
            num_scalar_prefetch=1,
            grid=(steps,),
            in_specs=[
                pl.BlockSpec((2, tile), lambda i, place: (0, i)),
                pl.BlockSpec((2, tile), lambda i, place: (0, i)),
                pl.BlockSpec((tile, width), lambda i, place: (i, 0)),
                pl.BlockSpec((tile, width), lambda i, place: (i, 0)),
            ],
            out_specs=[placed, placed],
            scratch_shapes=[pltpu.VMEM((tile, width), jnp.bfloat16)],
        ),
        out_shape=[jax.ShapeDtypeStruct((count // 2, width), jnp.bfloat16)] * 2,
        compiler_params=pltpu.CompilerParams(vmem_limit_bytes=24 << 20),
        name="scaled",
    )(place, local_stats, whole_stats, out_all, target_all)
    received = from_ahead(theirs, "core", 1)
    merged = (mine.astype(jnp.float32) + received.astype(jnp.float32)).astype(jnp.bfloat16)
    pieces = lax.all_to_all(merged, CHIPS, split_axis=0, concat_axis=0, tiled=True)
    back = jnp.sum(pieces.reshape(-1, queries.shape[0], width).astype(jnp.float32), axis=0)
    back_low = back.astype(jnp.bfloat16)
    query_grad = (
        back
        + lax.dot_general(back_low, adapter_w, (((1,), (1,)), ((), ())), preferred_element_type=jnp.float32)
    ).astype(jnp.bfloat16)
    b_own = spread_axes(back_low, CHIPS)
    b_other = from_ahead(b_own, "core", 1)
    third = width // 3
    column = pl.BlockSpec((tile, third), lambda i, place: (0, i))
    adapter_grad = pl.pallas_call(
        adapter_kernel,
        grid_spec=pltpu.PrefetchScalarGridSpec(
            num_scalar_prefetch=1,
            grid=(3,),
            in_specs=[column, column, column, column, WHOLE, WHOLE],
            out_specs=pl.BlockSpec((third, width), lambda i, place: (i, 0)),
            scratch_shapes=[
                pltpu.VMEM((count, third), jnp.bfloat16),
                pltpu.VMEM((count, width), jnp.bfloat16),
            ],
        ),
        out_shape=jax.ShapeDtypeStruct((width, width), jnp.float32),
        compiler_params=pltpu.CompilerParams(vmem_limit_bytes=24 << 20),
        cost_estimate=pl.CostEstimate(
            flops=2 * count * width * width, bytes_accessed=count * width * 4, transcendentals=0
        ),
        name="adapter",
    )(place, *gathered, b_own, b_other)
    return (query_grad, adapter_grad)


def solution(mesh):
    split = Mesh(mesh.devices.reshape(SIZES), AXES)
    placed = (
        P(AXES, None),
        P(),
        P(("z", "core"), ("y", "x"), None),
        P(AXES, None),
        P(),
        P(),
        P(AXES),
    )
    return jax.shard_map(
        all_steps,
        mesh=split,
        in_specs=placed,
        out_specs=(P(AXES, None), P()),
        check_vma=False,
    )
```

```python
import functools
import math

import jax
import jax.numpy as jnp
from jax import lax
from jax.experimental import pallas as pl
from jax.experimental.pallas import tpu as pltpu
from jax.sharding import Mesh
from jax.sharding import PartitionSpec as P

ROWS = 128
NEG_FILL = -1e30
LANES = 128
PROBES = 16
SIZES = (4, 2, 4, 4)
AXES = ("z", "core", "y", "x")
CHIPS = ("z", "y", "x")
ORDER = (0, 1, 3, 2)
LOG2E = 1.4426950408889634
WHOLE = pl.BlockSpec(memory_space=pltpu.VMEM)


def from_ahead(value, axis, step):
    size = lax.axis_size(axis)
    return lax.ppermute(value, axis, [((i + step) % size, i) for i in range(size)])


def chunk_of(i):
    return jnp.where(i < 2, i, 5 - i)


def spread_axes(value, axes):
    size = lax.axis_size(axes)
    spread = jnp.broadcast_to(value[None], (size,) + value.shape).reshape((-1,) + value.shape[1:])
    return lax.all_to_all(spread, axes, split_axis=0, concat_axis=0, tiled=True)


def lanes_of(column, tile):
    return jnp.broadcast_to(column, (tile, LANES))


def columns_of(rows, tile):
    return jnp.concatenate([rows, jnp.zeros((LANES - rows.shape[0], tile), jnp.float32)], axis=0).T


def score_kernel(
    table, place, own_ref, other_ref, w_ref, rows_ref,
    p_ref, tops_ref, stats_ref, code_ref, q_out, q_ref, bias_ref, s_ref, here_ref,
):
    width = w_ref.shape[0]
    tile = own_ref.shape[0]
    lists, per = rows_ref.shape[0], rows_ref.shape[1]
    factor = LOG2E / math.sqrt(width)
    core = pl.program_id(0)

    def find(n, _):
        at = place[4 + n] - place[2]
        here_ref[jnp.where((at >= 0) & (at < lists), at, lists)] = n
        return 0

    lax.fori_loop(0, table, find, 0)
    here = [here_ref[j] for j in range(lists)]
    total_rows = [ROWS * place[4 + table + n] for n in here]
    live = [n - place[3] for n in total_rows]

    @pl.when(core == place[1])
    def _():
        q_ref[...] = own_ref[...]

    @pl.when(core != place[1])
    def _():
        q_ref[...] = other_ref[...]

    queries = q_ref[:, :width]
    q_out[...] = queries.astype(jnp.float32).T.astype(jnp.bfloat16)
    info = q_ref[:, width:].astype(jnp.float32).T
    probes = info[0:PROBES, :]
    number = lax.broadcasted_iota(jnp.int32, (PROBES, tile), 0).astype(jnp.float32)
    target = jnp.sum(jnp.where(number == info[PROBES : PROBES + 1, :], probes, 0.0), axis=0, keepdims=True)
    raw_row = info[PROBES + 1 : PROBES + 2, :] * 64.0 + info[PROBES + 2 : PROBES + 3, :]
    code = jnp.full((1, tile), -1.0, jnp.float32)
    bias = []
    for j in range(lists):
        name = here[j].astype(jnp.float32)
        probed = jnp.max(jnp.where(probes == name, 1.0, 0.0), axis=0, keepdims=True)
        bias.append(jnp.where(probed > 0.0, 0.0, NEG_FILL))
        length = total_rows[j].astype(jnp.float32)
        row = raw_row - jnp.where(raw_row >= length, length, 0.0) - place[3].astype(jnp.float32)
        inside = (target == name) & (row >= 0.0) & (row < float(per))
        code = jnp.where(inside, row + float(j * per), code)
    code_ref[...] = code
    bias = columns_of(jnp.concatenate(bias, axis=0), tile)
    for j in range(lists):
        bias_ref[j] = lanes_of(bias[:, j : j + 1], tile)
    bias_ref[lists] = jnp.full((tile, LANES), NEG_FILL, jnp.float32)

    adapted = (
        queries.astype(jnp.float32) + jnp.dot(queries, w_ref[...], preferred_element_type=jnp.float32)
    ).astype(jnp.bfloat16)

    lane = lax.broadcasted_iota(jnp.int32, (tile, LANES), 1)
    blocks = per // LANES
    rows_at = pl.ds(pl.multiple_of(core * tile, tile), tile)

    def matmul(j):
        raw = lax.dot_general(
            adapted, rows_ref[j], (((1,), (1,)), ((), ())), preferred_element_type=jnp.float32
        )
        top = None
        for b in range(blocks):
            which = jnp.where(live[j] > b * LANES, j, lists)
            piece = raw[:, b * LANES : (b + 1) * LANES] + bias_ref[which]
            s_ref[j % 2, :, b * LANES : (b + 1) * LANES] = piece
            top = piece if top is None else jnp.maximum(top, piece)
        return top

    def weigh(j, top):
        peak = lanes_of(jnp.max(top, axis=1, keepdims=True), tile) * factor
        total = None
        for b in range(blocks):
            weight = jnp.exp2(s_ref[j % 2, :, b * LANES : (b + 1) * LANES] * factor - peak)
            total = weight if total is None else total + weight
            at = j * per + b * LANES
            p_ref[rows_at, at : at + LANES] = weight.astype(jnp.bfloat16)
        return peak, lanes_of(jnp.sum(total, axis=1, keepdims=True), tile)

    tops = jnp.full((tile, LANES), NEG_FILL, jnp.float32)
    sums = jnp.zeros((tile, LANES), jnp.float32)
    waiting = matmul(0)
    for j in range(lists):
        following = matmul(j + 1) if j + 1 < lists else None
        peak, total = weigh(j, waiting)
        tops = jnp.where(lane == j, peak, tops)
        sums = jnp.where(lane == j, total, sums)
        waiting = following
    tops = tops.T[0:lists, :]
    sums = sums.T[0:lists, :]
    tops_ref[...] = tops
    high = jnp.max(tops, axis=0, keepdims=True)
    stats_ref[0:1, :] = high
    stats_ref[1:2, :] = jnp.sum(sums * jnp.exp2(tops - high), axis=0, keepdims=True)


def back_kernel(stats_ref, code_ref, tops_ref, p_ref, rows_ref, *refs):
    out_ref, target_ref, g_ref, row_ref = refs[-4:]
    lists, per, width = rows_ref.shape
    tile = tops_ref.shape[1]
    rows_at = pl.ds(pl.multiple_of(pl.program_id(0) * tile, tile), tile)
    share = columns_of(jnp.exp2(tops_ref[...] - stats_ref[0:1, :]), tile)
    acc = None
    for j in range(lists):
        part = lanes_of(share[:, j : j + 1], tile)
        for b in range(per // LANES):
            at = j * per + b * LANES
            g_ref[:, at : at + LANES] = (p_ref[rows_at, at : at + LANES].astype(jnp.float32) * part).astype(jnp.bfloat16)
        out = jnp.dot(g_ref[:, j * per : (j + 1) * per], rows_ref[j], preferred_element_type=jnp.float32)
        acc = out if acc is None else acc + out
    out_ref[...] = acc

    row_ref[...] = jnp.zeros_like(row_ref)
    code = code_ref[...]
    index = lax.broadcasted_iota(jnp.int32, (1, tile), 1).astype(jnp.float32)
    sub = lax.broadcasted_iota(jnp.int32, (16, width), 0)
    none = float(tile)

    def first_after(last):
        return jnp.min(jnp.where((code >= 0.0) & (index > last), index, none))

    def step(at):
        key = jnp.max(jnp.where(index == at, code, -1.0)).astype(jnp.int32)
        group = rows_ref[key // per, pl.ds(pl.multiple_of((key % per) // 16 * 16, 16), 16), :]
        row = jnp.sum(jnp.where(sub == key % 16, group.astype(jnp.float32), 0.0), axis=0, keepdims=True)
        row_ref[pl.ds(at.astype(jnp.int32), 1), :] = row
        return first_after(at)

    lax.while_loop(lambda at: at < none, step, first_after(-1.0))
    target_ref[...] = row_ref[...].astype(jnp.bfloat16)


def scale_kernel(place, local_ref, whole_ref, out_ref, target_ref, mine_ref, theirs_ref, r_ref):
    tile, width = out_ref.shape
    half = tile // 2
    share = jnp.exp2(local_ref[0:1, :] - whole_ref[0:1, :]) / whole_ref[1:2, :]
    share = jnp.broadcast_to(share, (LANES, tile)).T
    for b in range(width // LANES):
        at = slice(b * LANES, (b + 1) * LANES)
        r_ref[:, at] = (
            (out_ref[:, at] * share - target_ref[:, at].astype(jnp.float32)) * (1.0 / math.sqrt(width))
        ).astype(jnp.bfloat16)
    mine_ref[...] = r_ref[pl.ds(pl.multiple_of(place[1] * half, half), half), :]
    theirs_ref[...] = r_ref[pl.ds(pl.multiple_of((1 - place[1]) * half, half), half), :]


def adapter_kernel(place, q0, q1, q2, q3, b_own, b_other, out_ref, q_ref, b_ref):
    tile = q0.shape[1]
    half = tile // 2
    count = 4 * tile

    @pl.when(pl.program_id(0) == 0)
    def _():
        for i in range(4):
            for source, core in ((b_own, place[1]), (b_other, 1 - place[1])):
                to = pl.multiple_of(i * tile + core * half, half)
                b_ref[pl.ds(to, half), :] = source[i * half : (i + 1) * half, :]

    for ahead, q in zip(ORDER, (q0, q1, q2, q3)):
        to = pl.multiple_of(lax.rem(place[0] + ahead, 4) * tile, tile)
        q_ref[:, pl.ds(to, tile)] = q[...]
    out_ref[...] = jnp.dot(q_ref[...], b_ref[...], preferred_element_type=jnp.float32) * (1.0 / math.sqrt(count))


def merge_axis(stats, axis):
    chunk = stats.shape[1] // 4
    parts = [stats]
    for j in range(1, lax.axis_size(axis)):
        part = from_ahead(stats, axis, j)
        if axis == "z":
            at = [ORDER.index((ahead - j) % 4) for ahead in ORDER]
            part = jnp.concatenate([part[:, k * chunk : (k + 1) * chunk] for k in at], axis=1)
        parts.append(part)
    top = functools.reduce(jnp.maximum, [p[0] for p in parts])
    total = sum(p[1] * jnp.exp2(p[0] - top) for p in parts)
    return jnp.stack([top, total])


def all_steps(queries, adapter_w, index_rows, probes, list_slot, block_counts, target_raw):
    width = queries.shape[1]
    lists_here, rows_here = index_rows.shape[0], index_rows.shape[1]
    place_z, place_c = lax.axis_index("z"), lax.axis_index("core")
    place_y, place_x = lax.axis_index("y"), lax.axis_index("x")
    first_slot = (place_z * 2 + place_c) * lists_here
    first_row = (place_y * 4 + place_x) * rows_here
    list_length = rows_here * 16
    table = list_slot.shape[0]
    place = jnp.concatenate(
        [jnp.stack([place_z, place_c, first_slot, first_row]).astype(jnp.int32), list_slot, block_counts]
    )

    lane = jnp.arange(LANES, dtype=jnp.int32)[None, :]
    raw_row = lax.rem(target_raw, list_length)[:, None]
    info = jnp.pad(probes, ((0, 0), (0, LANES - PROBES)))
    info = jnp.where(lane == PROBES, lax.div(target_raw, list_length)[:, None], info)
    info = jnp.where(lane == PROBES + 1, lax.div(raw_row, 64), info)
    info = jnp.where(lane == PROBES + 2, lax.rem(raw_row, 64), info)
    packed = jnp.concatenate([queries, info.astype(jnp.bfloat16)], axis=1)
    packed, place = lax.optimization_barrier((packed, place))
    plane = spread_axes(packed, ("y", "x"))

    half = plane.shape[0]
    tile = 2 * half
    steps = 4
    count = steps * tile
    keys = lists_here * rows_here
    owns = [plane]
    for ahead in ORDER[1:]:
        owns.append(from_ahead(plane, "z", ahead))
    weights, tops, stats, codes, gathered = [], [], [], [], []
    for ahead, own in zip(ORDER, owns):
        other = from_ahead(own, "core", 1)
        call = pl.pallas_call(
            functools.partial(score_kernel, table),
            grid_spec=pltpu.PrefetchScalarGridSpec(
                num_scalar_prefetch=1,
                grid=(2,),
                in_specs=[
                    pl.BlockSpec((half, width + LANES), lambda i, *_: (0, 0)),
                    pl.BlockSpec((half, width + LANES), lambda i, *_: (0, 0)),
                    WHOLE,
                    WHOLE,
                ],
                out_specs=[
                    WHOLE,
                    pl.BlockSpec((lists_here, half), lambda i, *_: (0, i)),
                    pl.BlockSpec((2, half), lambda i, *_: (0, i)),
                    pl.BlockSpec((1, half), lambda i, *_: (0, i)),
                    pl.BlockSpec((width, half), lambda i, *_: (0, i)),
                ],
                scratch_shapes=[
                    pltpu.VMEM((half, width + LANES), jnp.bfloat16),
                    pltpu.VMEM((lists_here + 1, half, LANES), jnp.float32),
                    pltpu.VMEM((2, half, rows_here), jnp.float32),
                    pltpu.SMEM((lists_here + 1,), jnp.int32),
                ],
            ),
            out_shape=[
                jax.ShapeDtypeStruct((tile, keys), jnp.bfloat16),
                jax.ShapeDtypeStruct((lists_here, tile), jnp.float32),
                jax.ShapeDtypeStruct((2, tile), jnp.float32),
                jax.ShapeDtypeStruct((1, tile), jnp.float32),
                jax.ShapeDtypeStruct((width, tile), jnp.bfloat16),
            ],
            compiler_params=pltpu.CompilerParams(vmem_limit_bytes=16 << 20),
            cost_estimate=pl.CostEstimate(
                flops=2 * tile * width * (keys + width), bytes_accessed=tile * keys * 2, transcendentals=tile * keys
            ),
            name="scores",
        )
        outs = call(place, own, other, adapter_w, index_rows)
        for kept, value in zip((weights, tops, stats, codes, gathered), outs):
            kept.append(value)

    out_all = target_all = None
    for i in range(steps):
        rest = [] if i == 0 else [out_all, target_all]
        out_all, target_all = pl.pallas_call(
            back_kernel,
            grid=(2,),
            in_specs=[
                pl.BlockSpec((2, half), lambda k: (0, k)),
                pl.BlockSpec((1, half), lambda k: (0, k)),
                pl.BlockSpec((lists_here, half), lambda k: (0, k)),
                WHOLE,
                WHOLE,
            ]
            + [pl.BlockSpec(memory_space=pl.ANY)] * len(rest),
            out_specs=[pl.BlockSpec((half, width), lambda k, i=i: (2 * i + k, 0))] * 2,
            out_shape=[
                jax.ShapeDtypeStruct((count, width), jnp.float32),
                jax.ShapeDtypeStruct((count, width), jnp.bfloat16),
            ],
            scratch_shapes=[
                pltpu.VMEM((half, keys), jnp.bfloat16),
                pltpu.VMEM((half, width), jnp.float32),
            ],
            input_output_aliases={5: 0, 6: 1} if rest else {},
            compiler_params=pltpu.CompilerParams(vmem_limit_bytes=24 << 20),
            cost_estimate=pl.CostEstimate(
                flops=2 * tile * width * keys, bytes_accessed=tile * keys * 2, transcendentals=0
            ),
            name="backs",
        )(stats[i], codes[i], tops[i], weights[i], index_rows, *rest)

    local_stats = jnp.concatenate(stats, axis=1)
    whole_stats = local_stats
    for axis in ("core", "x", "y", "z"):
        whole_stats = merge_axis(whole_stats, axis)

    placed = pl.BlockSpec((half, width), lambda i, place: (lax.rem(place[0] + chunk_of(i), 4), 0))
    mine, theirs = pl.pallas_call(
        scale_kernel,
        grid_spec=pltpu.PrefetchScalarGridSpec(
            num_scalar_prefetch=1,
            grid=(steps,),
            in_specs=[
                pl.BlockSpec((2, tile), lambda i, place: (0, i)),
                pl.BlockSpec((2, tile), lambda i, place: (0, i)),
                pl.BlockSpec((tile, width), lambda i, place: (i, 0)),
                pl.BlockSpec((tile, width), lambda i, place: (i, 0)),
            ],
            out_specs=[placed, placed],
            scratch_shapes=[pltpu.VMEM((tile, width), jnp.bfloat16)],
        ),
        out_shape=[jax.ShapeDtypeStruct((count // 2, width), jnp.bfloat16)] * 2,
        compiler_params=pltpu.CompilerParams(vmem_limit_bytes=24 << 20),
        name="scaled",
    )(place, local_stats, whole_stats, out_all, target_all)
    received = from_ahead(theirs, "core", 1)
    merged = (mine.astype(jnp.float32) + received.astype(jnp.float32)).astype(jnp.bfloat16)
    pieces = lax.all_to_all(merged, CHIPS, split_axis=0, concat_axis=0, tiled=True)
    back = jnp.sum(pieces.reshape(-1, queries.shape[0], width).astype(jnp.float32), axis=0)
    back_low = back.astype(jnp.bfloat16)
    query_grad = (
        back
        + lax.dot_general(back_low, adapter_w, (((1,), (1,)), ((), ())), preferred_element_type=jnp.float32)
    ).astype(jnp.bfloat16)
    b_own = spread_axes(back_low, CHIPS)
    b_other = from_ahead(b_own, "core", 1)
    third = width // 3
    column = pl.BlockSpec((third, tile), lambda i, place: (i, 0))
    adapter_grad = pl.pallas_call(
        adapter_kernel,
        grid_spec=pltpu.PrefetchScalarGridSpec(
            num_scalar_prefetch=1,
            grid=(3,),
            in_specs=[column, column, column, column, WHOLE, WHOLE],
            out_specs=pl.BlockSpec((third, width), lambda i, place: (i, 0)),
            scratch_shapes=[
                pltpu.VMEM((third, count), jnp.bfloat16),
                pltpu.VMEM((count, width), jnp.bfloat16),
            ],
        ),
        out_shape=jax.ShapeDtypeStruct((width, width), jnp.float32),
        compiler_params=pltpu.CompilerParams(vmem_limit_bytes=24 << 20),
        cost_estimate=pl.CostEstimate(
            flops=2 * count * width * width, bytes_accessed=count * width * 4, transcendentals=0
        ),
        name="adapter",
    )(place, *gathered, b_own, b_other)
    return (query_grad, adapter_grad)


def solution(mesh):
    split = Mesh(mesh.devices.reshape(SIZES), AXES)
    placed = (
        P(AXES, None),
        P(),
        P(("z", "core"), ("y", "x"), None),
        P(AXES, None),
        P(),
        P(),
        P(AXES),
    )
    return jax.shard_map(
        all_steps,
        mesh=split,
        in_specs=placed,
        out_specs=(P(AXES, None), P()),
        check_vma=False,
    )
```

```python
import functools
import math

import jax
import jax.numpy as jnp
from jax import lax
from jax.experimental import pallas as pl
from jax.experimental.pallas import tpu as pltpu
from jax.sharding import Mesh
from jax.sharding import PartitionSpec as P

ROWS = 128
NEG_FILL = -1e30
LANES = 128
PROBES = 16
SIZES = (4, 2, 4, 4)
AXES = ("z", "core", "y", "x")
CHIPS = ("z", "y", "x")
ORDER = (0, 1, 3, 2)
LOG2E = 1.4426950408889634
WHOLE = pl.BlockSpec(memory_space=pltpu.VMEM)


def from_ahead(value, axis, step):
    size = lax.axis_size(axis)
    return lax.ppermute(value, axis, [((i + step) % size, i) for i in range(size)])


def chunk_of(i):
    return jnp.where(i < 2, i, 5 - i)


def spread_axes(value, axes):
    size = lax.axis_size(axes)
    spread = jnp.broadcast_to(value[None], (size,) + value.shape).reshape((-1,) + value.shape[1:])
    return lax.all_to_all(spread, axes, split_axis=0, concat_axis=0, tiled=True)


def lanes_of(column, tile):
    return jnp.broadcast_to(column, (tile, LANES))


def columns_of(rows, tile):
    return jnp.concatenate([rows, jnp.zeros((LANES - rows.shape[0], tile), jnp.float32)], axis=0).T


def score_kernel(
    table, place, own_ref, other_ref, w_ref, rows_ref,
    p_ref, tops_ref, stats_ref, code_ref, q_out, q_ref, bias_ref, s_ref, here_ref,
):
    width = w_ref.shape[0]
    tile = own_ref.shape[0]
    lists, per = rows_ref.shape[0], rows_ref.shape[1]
    factor = LOG2E / math.sqrt(width)
    core = pl.program_id(0)

    def find(n, _):
        at = place[4 + n] - place[2]
        here_ref[jnp.where((at >= 0) & (at < lists), at, lists)] = n
        return 0

    lax.fori_loop(0, table, find, 0)
    here = [here_ref[j] for j in range(lists)]
    total_rows = [ROWS * place[4 + table + n] for n in here]
    live = [n - place[3] for n in total_rows]

    @pl.when(core == place[1])
    def _():
        q_ref[...] = own_ref[...]

    @pl.when(core != place[1])
    def _():
        q_ref[...] = other_ref[...]

    queries = q_ref[:, :width]
    q_out[...] = queries.astype(jnp.float32).T.astype(jnp.bfloat16)
    info = q_ref[:, width:].astype(jnp.float32).T
    probes = info[0:PROBES, :]
    number = lax.broadcasted_iota(jnp.int32, (PROBES, tile), 0).astype(jnp.float32)
    target = jnp.sum(jnp.where(number == info[PROBES : PROBES + 1, :], probes, 0.0), axis=0, keepdims=True)
    raw_row = info[PROBES + 1 : PROBES + 2, :] * 64.0 + info[PROBES + 2 : PROBES + 3, :]
    code = jnp.full((1, tile), -1.0, jnp.float32)
    bias = []
    for j in range(lists):
        name = here[j].astype(jnp.float32)
        probed = jnp.max(jnp.where(probes == name, 1.0, 0.0), axis=0, keepdims=True)
        bias.append(jnp.where(probed > 0.0, 0.0, NEG_FILL))
        length = total_rows[j].astype(jnp.float32)
        row = raw_row - jnp.where(raw_row >= length, length, 0.0) - place[3].astype(jnp.float32)
        inside = (target == name) & (row >= 0.0) & (row < float(per))
        code = jnp.where(inside, row + float(j * per), code)
    code_ref[...] = code
    bias = columns_of(jnp.concatenate(bias, axis=0), tile)
    for j in range(lists):
        bias_ref[j] = lanes_of(bias[:, j : j + 1], tile)
    bias_ref[lists] = jnp.full((tile, LANES), NEG_FILL, jnp.float32)

    adapted = (
        queries.astype(jnp.float32) + jnp.dot(queries, w_ref[...], preferred_element_type=jnp.float32)
    ).astype(jnp.bfloat16)

    lane = lax.broadcasted_iota(jnp.int32, (tile, LANES), 1)
    blocks = per // LANES

    def matmul(j):
        raw = lax.dot_general(
            adapted, rows_ref[j], (((1,), (1,)), ((), ())), preferred_element_type=jnp.float32
        )
        top = None
        for b in range(blocks):
            which = jnp.where(live[j] > b * LANES, j, lists)
            piece = raw[:, b * LANES : (b + 1) * LANES] + bias_ref[which]
            s_ref[j % 2, :, b * LANES : (b + 1) * LANES] = piece
            top = piece if top is None else jnp.maximum(top, piece)
        return top

    def weigh(j, top):
        peak = lanes_of(jnp.max(top, axis=1, keepdims=True), tile) * factor
        total = None
        for b in range(blocks):
            weight = jnp.exp2(s_ref[j % 2, :, b * LANES : (b + 1) * LANES] * factor - peak)
            total = weight if total is None else total + weight
            at = j * per + b * LANES
            p_ref[:, at : at + LANES] = weight.astype(jnp.bfloat16)
        return peak, lanes_of(jnp.sum(total, axis=1, keepdims=True), tile)

    tops = jnp.full((tile, LANES), NEG_FILL, jnp.float32)
    sums = jnp.zeros((tile, LANES), jnp.float32)
    waiting = matmul(0)
    for j in range(lists):
        following = matmul(j + 1) if j + 1 < lists else None
        peak, total = weigh(j, waiting)
        tops = jnp.where(lane == j, peak, tops)
        sums = jnp.where(lane == j, total, sums)
        waiting = following
    tops = tops.T[0:lists, :]
    sums = sums.T[0:lists, :]
    tops_ref[...] = tops
    high = jnp.max(tops, axis=0, keepdims=True)
    stats_ref[0:1, :] = high
    stats_ref[1:2, :] = jnp.sum(sums * jnp.exp2(tops - high), axis=0, keepdims=True)


def back_kernel(stats_ref, code_ref, tops_ref, p_ref, rows_ref, *refs):
    out_ref, target_ref, g_ref, row_ref = refs[-4:]
    lists, per, width = rows_ref.shape
    tile = tops_ref.shape[1]
    share = columns_of(jnp.exp2(tops_ref[...] - stats_ref[0:1, :]), tile)
    acc = None
    for j in range(lists):
        part = lanes_of(share[:, j : j + 1], tile)
        for b in range(per // LANES):
            at = j * per + b * LANES
            g_ref[:, at : at + LANES] = (p_ref[:, at : at + LANES].astype(jnp.float32) * part).astype(jnp.bfloat16)
        out = jnp.dot(g_ref[:, j * per : (j + 1) * per], rows_ref[j], preferred_element_type=jnp.float32)
        acc = out if acc is None else acc + out
    out_ref[...] = acc

    row_ref[...] = jnp.zeros_like(row_ref)
    code = code_ref[...]
    index = lax.broadcasted_iota(jnp.int32, (1, tile), 1).astype(jnp.float32)
    sub = lax.broadcasted_iota(jnp.int32, (16, width), 0)
    none = float(tile)

    def first_after(last):
        return jnp.min(jnp.where((code >= 0.0) & (index > last), index, none))

    def step(at):
        key = jnp.max(jnp.where(index == at, code, -1.0)).astype(jnp.int32)
        group = rows_ref[key // per, pl.ds(pl.multiple_of((key % per) // 16 * 16, 16), 16), :]
        row = jnp.sum(jnp.where(sub == key % 16, group.astype(jnp.float32), 0.0), axis=0, keepdims=True)
        row_ref[pl.ds(at.astype(jnp.int32), 1), :] = row
        return first_after(at)

    lax.while_loop(lambda at: at < none, step, first_after(-1.0))
    target_ref[...] = row_ref[...].astype(jnp.bfloat16)


def scale_kernel(place, local_ref, whole_ref, out_ref, target_ref, mine_ref, theirs_ref, r_ref):
    tile, width = out_ref.shape
    half = tile // 2
    share = jnp.exp2(local_ref[0:1, :] - whole_ref[0:1, :]) / whole_ref[1:2, :]
    share = jnp.broadcast_to(share, (LANES, tile)).T
    for b in range(width // LANES):
        at = slice(b * LANES, (b + 1) * LANES)
        r_ref[:, at] = (
            (out_ref[:, at] * share - target_ref[:, at].astype(jnp.float32)) * (1.0 / math.sqrt(width))
        ).astype(jnp.bfloat16)
    mine_ref[...] = r_ref[pl.ds(pl.multiple_of(place[1] * half, half), half), :]
    theirs_ref[...] = r_ref[pl.ds(pl.multiple_of((1 - place[1]) * half, half), half), :]


def adapter_kernel(place, q0, q1, q2, q3, b_own, b_other, out_ref, q_ref, b_ref):
    tile = q0.shape[1]
    half = tile // 2
    count = 4 * tile

    @pl.when(pl.program_id(0) == 0)
    def _():
        for i in range(4):
            for source, core in ((b_own, place[1]), (b_other, 1 - place[1])):
                to = pl.multiple_of(i * tile + core * half, half)
                b_ref[pl.ds(to, half), :] = source[i * half : (i + 1) * half, :]

    for ahead, q in zip(ORDER, (q0, q1, q2, q3)):
        to = pl.multiple_of(lax.rem(place[0] + ahead, 4) * tile, tile)
        q_ref[:, pl.ds(to, tile)] = q[...]
    out_ref[...] = jnp.dot(q_ref[...], b_ref[...], preferred_element_type=jnp.float32) * (1.0 / math.sqrt(count))


def merge_axis(stats, axis):
    chunk = stats.shape[1] // 4
    parts = [stats]
    for j in range(1, lax.axis_size(axis)):
        part = from_ahead(stats, axis, j)
        if axis == "z":
            at = [ORDER.index((ahead - j) % 4) for ahead in ORDER]
            part = jnp.concatenate([part[:, k * chunk : (k + 1) * chunk] for k in at], axis=1)
        parts.append(part)
    top = functools.reduce(jnp.maximum, [p[0] for p in parts])
    total = sum(p[1] * jnp.exp2(p[0] - top) for p in parts)
    return jnp.stack([top, total])


def all_steps(queries, adapter_w, index_rows, probes, list_slot, block_counts, target_raw):
    width = queries.shape[1]
    lists_here, rows_here = index_rows.shape[0], index_rows.shape[1]
    place_z, place_c = lax.axis_index("z"), lax.axis_index("core")
    place_y, place_x = lax.axis_index("y"), lax.axis_index("x")
    first_slot = (place_z * 2 + place_c) * lists_here
    first_row = (place_y * 4 + place_x) * rows_here
    list_length = rows_here * 16
    table = list_slot.shape[0]
    place = jnp.concatenate(
        [jnp.stack([place_z, place_c, first_slot, first_row]).astype(jnp.int32), list_slot, block_counts]
    )

    lane = jnp.arange(LANES, dtype=jnp.int32)[None, :]
    raw_row = lax.rem(target_raw, list_length)[:, None]
    info = jnp.pad(probes, ((0, 0), (0, LANES - PROBES)))
    info = jnp.where(lane == PROBES, lax.div(target_raw, list_length)[:, None], info)
    info = jnp.where(lane == PROBES + 1, lax.div(raw_row, 64), info)
    info = jnp.where(lane == PROBES + 2, lax.rem(raw_row, 64), info)
    packed = jnp.concatenate([queries, info.astype(jnp.bfloat16)], axis=1)
    packed, place = lax.optimization_barrier((packed, place))
    plane = spread_axes(packed, ("y", "x"))

    half = plane.shape[0]
    tile = 2 * half
    steps = 4
    count = steps * tile
    keys = lists_here * rows_here
    owns = [plane]
    for ahead in (1, 3):
        owns.append(from_ahead(plane, "z", ahead))
    weights, tops, stats, codes, gathered = [], [], [], [], []
    for i, ahead in enumerate(ORDER):
        if i == 1:
            held, codes[0] = lax.optimization_barrier((plane, codes[0]))
            owns.append(from_ahead(held, "z", 2))
        own = owns[i]
        other = from_ahead(own, "core", 1)
        call = pl.pallas_call(
            functools.partial(score_kernel, table),
            grid_spec=pltpu.PrefetchScalarGridSpec(
                num_scalar_prefetch=1,
                grid=(2,),
                in_specs=[
                    pl.BlockSpec((half, width + LANES), lambda i, *_: (0, 0)),
                    pl.BlockSpec((half, width + LANES), lambda i, *_: (0, 0)),
                    WHOLE,
                    WHOLE,
                ],
                out_specs=[
                    pl.BlockSpec((half, keys), lambda i, *_: (i, 0)),
                    pl.BlockSpec((lists_here, half), lambda i, *_: (0, i)),
                    pl.BlockSpec((2, half), lambda i, *_: (0, i)),
                    pl.BlockSpec((1, half), lambda i, *_: (0, i)),
                    pl.BlockSpec((width, half), lambda i, *_: (0, i)),
                ],
                scratch_shapes=[
                    pltpu.VMEM((half, width + LANES), jnp.bfloat16),
                    pltpu.VMEM((lists_here + 1, half, LANES), jnp.float32),
                    pltpu.VMEM((2, half, rows_here), jnp.float32),
                    pltpu.SMEM((lists_here + 1,), jnp.int32),
                ],
            ),
            out_shape=[
                jax.ShapeDtypeStruct((tile, keys), jnp.bfloat16),
                jax.ShapeDtypeStruct((lists_here, tile), jnp.float32),
                jax.ShapeDtypeStruct((2, tile), jnp.float32),
                jax.ShapeDtypeStruct((1, tile), jnp.float32),
                jax.ShapeDtypeStruct((width, tile), jnp.bfloat16),
            ],
            compiler_params=pltpu.CompilerParams(vmem_limit_bytes=12 << 20),
            cost_estimate=pl.CostEstimate(
                flops=2 * tile * width * (keys + width), bytes_accessed=tile * keys * 2, transcendentals=tile * keys
            ),
            name="scores",
        )
        outs = call(place, own, other, adapter_w, index_rows)
        for kept, value in zip((weights, tops, stats, codes, gathered), outs):
            kept.append(value)

    out_all = target_all = None
    for i in range(steps):
        rest = [] if i == 0 else [out_all, target_all]
        out_all, target_all = pl.pallas_call(
            back_kernel,
            grid=(2,),
            in_specs=[
                pl.BlockSpec((2, half), lambda k: (0, k)),
                pl.BlockSpec((1, half), lambda k: (0, k)),
                pl.BlockSpec((lists_here, half), lambda k: (0, k)),
                pl.BlockSpec((half, keys), lambda k: (k, 0)),
                WHOLE,
            ]
            + [pl.BlockSpec(memory_space=pl.ANY)] * len(rest),
            out_specs=[pl.BlockSpec((half, width), lambda k, i=i: (2 * i + k, 0))] * 2,
            out_shape=[
                jax.ShapeDtypeStruct((count, width), jnp.float32),
                jax.ShapeDtypeStruct((count, width), jnp.bfloat16),
            ],
            scratch_shapes=[
                pltpu.VMEM((half, keys), jnp.bfloat16),
                pltpu.VMEM((half, width), jnp.float32),
            ],
            input_output_aliases={5: 0, 6: 1} if rest else {},
            compiler_params=pltpu.CompilerParams(vmem_limit_bytes=24 << 20),
            cost_estimate=pl.CostEstimate(
                flops=2 * tile * width * keys, bytes_accessed=tile * keys * 2, transcendentals=0
            ),
            name="backs",
        )(stats[i], codes[i], tops[i], weights[i], index_rows, *rest)

    local_stats = jnp.concatenate(stats, axis=1)
    whole_stats = local_stats
    for axis in ("core", "x", "y", "z"):
        whole_stats = merge_axis(whole_stats, axis)

    placed = pl.BlockSpec((half, width), lambda i, place: (lax.rem(place[0] + chunk_of(i), 4), 0))
    mine, theirs = pl.pallas_call(
        scale_kernel,
        grid_spec=pltpu.PrefetchScalarGridSpec(
            num_scalar_prefetch=1,
            grid=(steps,),
            in_specs=[
                pl.BlockSpec((2, tile), lambda i, place: (0, i)),
                pl.BlockSpec((2, tile), lambda i, place: (0, i)),
                pl.BlockSpec((tile, width), lambda i, place: (i, 0)),
                pl.BlockSpec((tile, width), lambda i, place: (i, 0)),
            ],
            out_specs=[placed, placed],
            scratch_shapes=[pltpu.VMEM((tile, width), jnp.bfloat16)],
        ),
        out_shape=[jax.ShapeDtypeStruct((count // 2, width), jnp.bfloat16)] * 2,
        compiler_params=pltpu.CompilerParams(vmem_limit_bytes=24 << 20),
        name="scaled",
    )(place, local_stats, whole_stats, out_all, target_all)
    received = from_ahead(theirs, "core", 1)
    merged = (mine.astype(jnp.float32) + received.astype(jnp.float32)).astype(jnp.bfloat16)
    pieces = lax.all_to_all(merged, CHIPS, split_axis=0, concat_axis=0, tiled=True)
    back = jnp.sum(pieces.reshape(-1, queries.shape[0], width).astype(jnp.float32), axis=0)
    back_low = back.astype(jnp.bfloat16)
    query_grad = (
        back
        + lax.dot_general(back_low, adapter_w, (((1,), (1,)), ((), ())), preferred_element_type=jnp.float32)
    ).astype(jnp.bfloat16)
    b_own = spread_axes(back_low, CHIPS)
    b_other = from_ahead(b_own, "core", 1)
    third = width // 3
    column = pl.BlockSpec((third, tile), lambda i, place: (i, 0))
    adapter_grad = pl.pallas_call(
        adapter_kernel,
        grid_spec=pltpu.PrefetchScalarGridSpec(
            num_scalar_prefetch=1,
            grid=(3,),
            in_specs=[column, column, column, column, WHOLE, WHOLE],
            out_specs=pl.BlockSpec((third, width), lambda i, place: (i, 0)),
            scratch_shapes=[
                pltpu.VMEM((third, count), jnp.bfloat16),
                pltpu.VMEM((count, width), jnp.bfloat16),
            ],
        ),
        out_shape=jax.ShapeDtypeStruct((width, width), jnp.float32),
        compiler_params=pltpu.CompilerParams(vmem_limit_bytes=24 << 20),
        cost_estimate=pl.CostEstimate(
            flops=2 * count * width * width, bytes_accessed=count * width * 4, transcendentals=0
        ),
        name="adapter",
    )(place, *gathered, b_own, b_other)
    return (query_grad, adapter_grad)


def solution(mesh):
    split = Mesh(mesh.devices.reshape(SIZES), AXES)
    placed = (
        P(AXES, None),
        P(),
        P(("z", "core"), ("y", "x"), None),
        P(AXES, None),
        P(),
        P(),
        P(AXES),
    )
    return jax.shard_map(
        all_steps,
        mesh=split,
        in_specs=placed,
        out_specs=(P(AXES, None), P()),
        check_vma=False,
    )
```

```python
import functools
import math

import jax
import jax.numpy as jnp
from jax import lax
from jax.experimental import pallas as pl
from jax.experimental.pallas import tpu as pltpu
from jax.sharding import Mesh
from jax.sharding import PartitionSpec as P

ROWS = 128
NEG_FILL = -1e30
LANES = 128
PROBES = 16
SIZES = (4, 2, 4, 4)
AXES = ("z", "core", "y", "x")
CHIPS = ("z", "y", "x")
ORDER = (0, 1, 3, 2)
LOG2E = 1.4426950408889634
WHOLE = pl.BlockSpec(memory_space=pltpu.VMEM)


def from_ahead(value, axis, step):
    size = lax.axis_size(axis)
    return lax.ppermute(value, axis, [((i + step) % size, i) for i in range(size)])


def chunk_of(i):
    return jnp.where(i < 2, i, 5 - i)


def spread_axes(value, axes):
    size = lax.axis_size(axes)
    spread = jnp.broadcast_to(value[None], (size,) + value.shape).reshape((-1,) + value.shape[1:])
    return lax.all_to_all(spread, axes, split_axis=0, concat_axis=0, tiled=True)


def lanes_of(column, tile):
    return jnp.broadcast_to(column, (tile, LANES))


def columns_of(rows, tile):
    return jnp.concatenate([rows, jnp.zeros((LANES - rows.shape[0], tile), jnp.float32)], axis=0).T


def score_kernel(
    table, place, own_ref, other_ref, w_ref, rows_ref,
    p_ref, tops_ref, stats_ref, code_ref, q_out, q_ref, bias_ref, s_ref, here_ref,
):
    width = w_ref.shape[0]
    tile = own_ref.shape[0]
    lists, per = rows_ref.shape[0], rows_ref.shape[1]
    factor = LOG2E / math.sqrt(width)
    core = pl.program_id(0)

    @pl.when(core == 0)
    def _():
        for n in range(table):
            at = place[4 + n] - place[2]
            here_ref[jnp.where((at >= 0) & (at < lists), at, lists)] = n

    here = [here_ref[j] for j in range(lists)]
    total_rows = [ROWS * place[4 + table + n] for n in here]
    live = [n - place[3] for n in total_rows]

    @pl.when(core == place[1])
    def _():
        q_ref[...] = own_ref[...]

    @pl.when(core != place[1])
    def _():
        q_ref[...] = other_ref[...]

    queries = q_ref[:, :width]
    q_out[...] = queries.astype(jnp.float32).T.astype(jnp.bfloat16)
    info = q_ref[:, width:].astype(jnp.float32).T
    probes = info[0:PROBES, :]
    number = lax.broadcasted_iota(jnp.int32, (PROBES, tile), 0).astype(jnp.float32)
    target = jnp.sum(jnp.where(number == info[PROBES : PROBES + 1, :], probes, 0.0), axis=0, keepdims=True)
    raw_row = info[PROBES + 1 : PROBES + 2, :] * 64.0 + info[PROBES + 2 : PROBES + 3, :]
    code = jnp.full((1, tile), -1.0, jnp.float32)
    bias = []
    for j in range(lists):
        name = here[j].astype(jnp.float32)
        probed = jnp.max(jnp.where(probes == name, 1.0, 0.0), axis=0, keepdims=True)
        bias.append(jnp.where(probed > 0.0, 0.0, NEG_FILL))
        length = total_rows[j].astype(jnp.float32)
        row = raw_row - jnp.where(raw_row >= length, length, 0.0) - place[3].astype(jnp.float32)
        inside = (target == name) & (row >= 0.0) & (row < float(per))
        code = jnp.where(inside, row + float(j * per), code)
    code_ref[...] = code
    bias = columns_of(jnp.concatenate(bias, axis=0), tile)
    for j in range(lists):
        bias_ref[j] = lanes_of(bias[:, j : j + 1], tile)
    bias_ref[lists] = jnp.full((tile, LANES), NEG_FILL, jnp.float32)

    adapted = (
        queries.astype(jnp.float32) + jnp.dot(queries, w_ref[...], preferred_element_type=jnp.float32)
    ).astype(jnp.bfloat16)

    lane = lax.broadcasted_iota(jnp.int32, (tile, LANES), 1)
    blocks = per // LANES

    def matmul(j):
        raw = lax.dot_general(
            adapted, rows_ref[j], (((1,), (1,)), ((), ())), preferred_element_type=jnp.float32
        )
        top = None
        for b in range(blocks):
            which = jnp.where(live[j] > b * LANES, j, lists)
            piece = raw[:, b * LANES : (b + 1) * LANES] + bias_ref[which]
            s_ref[j % 2, :, b * LANES : (b + 1) * LANES] = piece
            top = piece if top is None else jnp.maximum(top, piece)
        return top

    def weigh(j, top):
        peak = lanes_of(jnp.max(top, axis=1, keepdims=True), tile) * factor
        total = None
        for b in range(blocks):
            weight = jnp.exp2(s_ref[j % 2, :, b * LANES : (b + 1) * LANES] * factor - peak)
            total = weight if total is None else total + weight
            at = j * per + b * LANES
            p_ref[:, at : at + LANES] = weight.astype(jnp.bfloat16)
        return peak, lanes_of(jnp.sum(total, axis=1, keepdims=True), tile)

    tops = jnp.full((tile, LANES), NEG_FILL, jnp.float32)
    sums = jnp.zeros((tile, LANES), jnp.float32)
    waiting = matmul(0)
    for j in range(lists):
        following = matmul(j + 1) if j + 1 < lists else None
        peak, total = weigh(j, waiting)
        tops = jnp.where(lane == j, peak, tops)
        sums = jnp.where(lane == j, total, sums)
        waiting = following
    tops = tops.T[0:lists, :]
    sums = sums.T[0:lists, :]
    tops_ref[...] = tops
    high = jnp.max(tops, axis=0, keepdims=True)
    stats_ref[0:1, :] = high
    stats_ref[1:2, :] = jnp.sum(sums * jnp.exp2(tops - high), axis=0, keepdims=True)


def back_kernel(stats_ref, code_ref, tops_ref, p_ref, rows_ref, *refs):
    out_ref, target_ref, g_ref, row_ref = refs[-4:]
    lists, per, width = rows_ref.shape
    tile = tops_ref.shape[1]
    share = columns_of(jnp.exp2(tops_ref[...] - stats_ref[0:1, :]), tile)
    acc = None
    for j in range(lists):
        part = lanes_of(share[:, j : j + 1], tile)
        for b in range(per // LANES):
            at = j * per + b * LANES
            g_ref[:, at : at + LANES] = (p_ref[:, at : at + LANES].astype(jnp.float32) * part).astype(jnp.bfloat16)
        out = jnp.dot(g_ref[:, j * per : (j + 1) * per], rows_ref[j], preferred_element_type=jnp.float32)
        acc = out if acc is None else acc + out
    out_ref[...] = acc

    row_ref[...] = jnp.zeros_like(row_ref)
    code = code_ref[...]
    index = lax.broadcasted_iota(jnp.int32, (1, tile), 1).astype(jnp.float32)
    sub = lax.broadcasted_iota(jnp.int32, (16, width), 0)
    none = float(tile)

    def first_after(last):
        return jnp.min(jnp.where((code >= 0.0) & (index > last), index, none))

    def step(at):
        key = jnp.max(jnp.where(index == at, code, -1.0)).astype(jnp.int32)
        group = rows_ref[key // per, pl.ds(pl.multiple_of((key % per) // 16 * 16, 16), 16), :]
        row = jnp.sum(jnp.where(sub == key % 16, group.astype(jnp.float32), 0.0), axis=0, keepdims=True)
        row_ref[pl.ds(at.astype(jnp.int32), 1), :] = row
        return first_after(at)

    lax.while_loop(lambda at: at < none, step, first_after(-1.0))
    target_ref[...] = row_ref[...].astype(jnp.bfloat16)


def scale_kernel(place, local_ref, whole_ref, out_ref, target_ref, scaled_ref):
    tile, width = out_ref.shape
    share = jnp.exp2(local_ref[0:1, :] - whole_ref[0:1, :]) / whole_ref[1:2, :]
    share = jnp.broadcast_to(share, (LANES, tile)).T
    for b in range(width // LANES):
        at = slice(b * LANES, (b + 1) * LANES)
        scaled_ref[:, at] = (
            (out_ref[:, at] * share - target_ref[:, at].astype(jnp.float32)) * (1.0 / math.sqrt(width))
        ).astype(jnp.bfloat16)


def adapter_kernel(other, place, q0, q1, q2, q3, b_ref, *refs):
    out_ref, q_ref = refs[-2:]
    half = b_ref.shape[0] // 4
    core = 1 - place[1] if other else place[1]
    for ahead, q in zip(ORDER, (q0, q1, q2, q3)):
        to = pl.multiple_of(lax.rem(place[0] + ahead, 4) * half, half)
        q_ref[:, pl.ds(to, half)] = q[:, pl.ds(pl.multiple_of(core * half, half), half)]
    total = jnp.dot(q_ref[...], b_ref[...], preferred_element_type=jnp.float32)
    if other:
        total = (total + refs[0][...]) * (1.0 / math.sqrt(8 * half))
    out_ref[...] = total


def merge_axis(stats, axis):
    chunk = stats.shape[1] // 4
    parts = [stats]
    for j in range(1, lax.axis_size(axis)):
        part = from_ahead(stats, axis, j)
        if axis == "z":
            at = [ORDER.index((ahead - j) % 4) for ahead in ORDER]
            part = jnp.concatenate([part[:, k * chunk : (k + 1) * chunk] for k in at], axis=1)
        parts.append(part)
    top = functools.reduce(jnp.maximum, [p[0] for p in parts])
    total = sum(p[1] * jnp.exp2(p[0] - top) for p in parts)
    return jnp.stack([top, total])


def all_steps(queries, adapter_w, index_rows, probes, list_slot, block_counts, target_raw):
    width = queries.shape[1]
    lists_here, rows_here = index_rows.shape[0], index_rows.shape[1]
    place_z, place_c = lax.axis_index("z"), lax.axis_index("core")
    place_y, place_x = lax.axis_index("y"), lax.axis_index("x")
    first_slot = (place_z * 2 + place_c) * lists_here
    first_row = (place_y * 4 + place_x) * rows_here
    list_length = rows_here * 16
    table = list_slot.shape[0]
    place = jnp.concatenate(
        [jnp.stack([place_z, place_c, first_slot, first_row]).astype(jnp.int32), list_slot, block_counts]
    )

    lane = jnp.arange(LANES, dtype=jnp.int32)[None, :]
    raw_row = lax.rem(target_raw, list_length)[:, None]
    info = jnp.pad(probes, ((0, 0), (0, LANES - PROBES)))
    info = jnp.where(lane == PROBES, lax.div(target_raw, list_length)[:, None], info)
    info = jnp.where(lane == PROBES + 1, lax.div(raw_row, 64), info)
    info = jnp.where(lane == PROBES + 2, lax.rem(raw_row, 64), info)
    packed = jnp.concatenate([queries, info.astype(jnp.bfloat16)], axis=1)
    packed, place = lax.optimization_barrier((packed, place))
    plane = spread_axes(packed, ("y", "x"))

    half = plane.shape[0]
    tile = 2 * half
    steps = 4
    count = steps * tile
    keys = lists_here * rows_here
    owns = [plane]
    for ahead in (1, 3):
        owns.append(from_ahead(plane, "z", ahead))
    weights, tops, stats, codes, gathered = [], [], [], [], []
    for i, ahead in enumerate(ORDER):
        if i == 1:
            held, codes[0] = lax.optimization_barrier((plane, codes[0]))
            owns.append(from_ahead(held, "z", 2))
        own = owns[i]
        other = from_ahead(own, "core", 1)
        call = pl.pallas_call(
            functools.partial(score_kernel, table),
            grid_spec=pltpu.PrefetchScalarGridSpec(
                num_scalar_prefetch=1,
                grid=(2,),
                in_specs=[
                    pl.BlockSpec((half, width + LANES), lambda i, *_: (0, 0)),
                    pl.BlockSpec((half, width + LANES), lambda i, *_: (0, 0)),
                    WHOLE,
                    WHOLE,
                ],
                out_specs=[
                    pl.BlockSpec((half, keys), lambda i, *_: (i, 0)),
                    pl.BlockSpec((lists_here, half), lambda i, *_: (0, i)),
                    pl.BlockSpec((2, half), lambda i, *_: (0, i)),
                    pl.BlockSpec((1, half), lambda i, *_: (0, i)),
                    pl.BlockSpec((width, half), lambda i, *_: (0, i)),
                ],
                scratch_shapes=[
                    pltpu.VMEM((half, width + LANES), jnp.bfloat16),
                    pltpu.VMEM((lists_here + 1, half, LANES), jnp.float32),
                    pltpu.VMEM((2, half, rows_here), jnp.float32),
                    pltpu.SMEM((lists_here + 1,), jnp.int32),
                ],
            ),
            out_shape=[
                jax.ShapeDtypeStruct((tile, keys), jnp.bfloat16),
                jax.ShapeDtypeStruct((lists_here, tile), jnp.float32),
                jax.ShapeDtypeStruct((2, tile), jnp.float32),
                jax.ShapeDtypeStruct((1, tile), jnp.float32),
                jax.ShapeDtypeStruct((width, tile), jnp.bfloat16),
            ],
            compiler_params=pltpu.CompilerParams(vmem_limit_bytes=12 << 20),
            cost_estimate=pl.CostEstimate(
                flops=2 * tile * width * (keys + width), bytes_accessed=tile * keys * 2, transcendentals=tile * keys
            ),
            name="scores",
        )
        outs = call(place, own, other, adapter_w, index_rows)
        for kept, value in zip((weights, tops, stats, codes, gathered), outs):
            kept.append(value)

    out_all = target_all = None
    for i in range(steps):
        rest = [] if i == 0 else [out_all, target_all]
        out_all, target_all = pl.pallas_call(
            back_kernel,
            grid=(2,),
            in_specs=[
                pl.BlockSpec((2, half), lambda k: (0, k)),
                pl.BlockSpec((1, half), lambda k: (0, k)),
                pl.BlockSpec((lists_here, half), lambda k: (0, k)),
                pl.BlockSpec((half, keys), lambda k: (k, 0)),
                WHOLE,
            ]
            + [pl.BlockSpec(memory_space=pl.ANY)] * len(rest),
            out_specs=[pl.BlockSpec((half, width), lambda k, i=i: (2 * i + k, 0))] * 2,
            out_shape=[
                jax.ShapeDtypeStruct((count, width), jnp.float32),
                jax.ShapeDtypeStruct((count, width), jnp.bfloat16),
            ],
            scratch_shapes=[
                pltpu.VMEM((half, keys), jnp.bfloat16),
                pltpu.VMEM((half, width), jnp.float32),
            ],
            input_output_aliases={5: 0, 6: 1} if rest else {},
            compiler_params=pltpu.CompilerParams(vmem_limit_bytes=24 << 20),
            cost_estimate=pl.CostEstimate(
                flops=2 * tile * width * keys, bytes_accessed=tile * keys * 2, transcendentals=0
            ),
            name="backs",
        )(stats[i], codes[i], tops[i], weights[i], index_rows, *rest)

    local_stats = jnp.concatenate(stats, axis=1)
    whole_stats = local_stats
    for axis in ("core", "x", "y", "z"):
        whole_stats = merge_axis(whole_stats, axis)

    def scaled(other):
        def part(i, place):
            return 2 * i + (1 - place[1] if other else place[1])

        return pl.pallas_call(
            scale_kernel,
            grid_spec=pltpu.PrefetchScalarGridSpec(
                num_scalar_prefetch=1,
                grid=(steps,),
                in_specs=[
                    pl.BlockSpec((2, half), lambda i, place: (0, part(i, place))),
                    pl.BlockSpec((2, half), lambda i, place: (0, part(i, place))),
                    pl.BlockSpec((half, width), lambda i, place: (part(i, place), 0)),
                    pl.BlockSpec((half, width), lambda i, place: (part(i, place), 0)),
                ],
                out_specs=pl.BlockSpec(
                    (half, width), lambda i, place: (lax.rem(place[0] + chunk_of(i), 4), 0)
                ),
            ),
            out_shape=jax.ShapeDtypeStruct((count // 2, width), jnp.bfloat16),
            compiler_params=pltpu.CompilerParams(vmem_limit_bytes=12 << 20),
            cost_estimate=pl.CostEstimate(
                flops=2 * count * width, bytes_accessed=count * width * 4, transcendentals=0
            ),
            name="scaled",
        )(place, local_stats, whole_stats, out_all, target_all)

    theirs = scaled(True)
    received = from_ahead(theirs, "core", 1)
    mine = scaled(False)
    merged = (mine.astype(jnp.float32) + received.astype(jnp.float32)).astype(jnp.bfloat16)
    pieces = lax.all_to_all(merged, CHIPS, split_axis=0, concat_axis=0, tiled=True)
    back = jnp.sum(pieces.reshape(-1, queries.shape[0], width).astype(jnp.float32), axis=0)
    back_low = back.astype(jnp.bfloat16)
    query_grad = (
        back
        + lax.dot_general(back_low, adapter_w, (((1,), (1,)), ((), ())), preferred_element_type=jnp.float32)
    ).astype(jnp.bfloat16)
    b_own = spread_axes(back_low, CHIPS)
    b_other = from_ahead(b_own, "core", 1)
    third = width // 3
    column = pl.BlockSpec((third, tile), lambda i, place: (i, 0))
    block = pl.BlockSpec((third, width), lambda i, place: (i, 0))

    def product(other, *rest):
        return pl.pallas_call(
            functools.partial(adapter_kernel, other),
            grid_spec=pltpu.PrefetchScalarGridSpec(
                num_scalar_prefetch=1,
                grid=(3,),
                in_specs=[column, column, column, column, WHOLE] + [block] * (len(rest) - 1),
                out_specs=block,
                scratch_shapes=[pltpu.VMEM((third, count // 2), jnp.bfloat16)],
            ),
            out_shape=jax.ShapeDtypeStruct((width, width), jnp.float32),
            compiler_params=pltpu.CompilerParams(vmem_limit_bytes=16 << 20),
            cost_estimate=pl.CostEstimate(
                flops=count * width * width, bytes_accessed=count * width * 2, transcendentals=0
            ),
            name="adapter",
        )(place, *gathered, *rest)

    partial = product(False, b_own)
    adapter_grad = product(True, b_other, partial)
    return (query_grad, adapter_grad)


def solution(mesh):
    split = Mesh(mesh.devices.reshape(SIZES), AXES)
    placed = (
        P(AXES, None),
        P(),
        P(("z", "core"), ("y", "x"), None),
        P(AXES, None),
        P(),
        P(),
        P(AXES),
    )
    return jax.shard_map(
        all_steps,
        mesh=split,
        in_specs=placed,
        out_specs=(P(AXES, None), P()),
        check_vma=False,
    )
```

```python
import functools
import math

import jax
import jax.numpy as jnp
from jax import lax
from jax.experimental import pallas as pl
from jax.experimental.pallas import tpu as pltpu
from jax.sharding import Mesh
from jax.sharding import PartitionSpec as P

ROWS = 128
NEG_FILL = -1e30
LANES = 128
PROBES = 16
SIZES = (4, 2, 4, 4)
AXES = ("z", "core", "y", "x")
CHIPS = ("z", "y", "x")
ORDER = (0, 1, 3, 2)
LOG2E = 1.4426950408889634
WHOLE = pl.BlockSpec(memory_space=pltpu.VMEM)


def from_ahead(value, axis, step):
    size = lax.axis_size(axis)
    return lax.ppermute(value, axis, [((i + step) % size, i) for i in range(size)])


def chunk_of(i):
    return jnp.where(i < 2, i, 5 - i)


def spread_axes(value, axes):
    size = lax.axis_size(axes)
    spread = jnp.broadcast_to(value[None], (size,) + value.shape).reshape((-1,) + value.shape[1:])
    return lax.all_to_all(spread, axes, split_axis=0, concat_axis=0, tiled=True)


def lanes_of(column, tile):
    return jnp.broadcast_to(column, (tile, LANES))


def columns_of(rows, tile):
    return jnp.concatenate([rows, jnp.zeros((LANES - rows.shape[0], tile), jnp.float32)], axis=0).T


def score_kernel(
    table, place, own_ref, other_ref, w_ref, rows_ref,
    p_ref, tops_ref, stats_ref, code_ref, q_out, q_ref, bias_ref, s_ref, here_ref,
):
    width = w_ref.shape[0]
    tile = own_ref.shape[0]
    lists, per = rows_ref.shape[0], rows_ref.shape[1]
    factor = LOG2E / math.sqrt(width)
    core = pl.program_id(0)

    @pl.when(core == 0)
    def _():
        for n in range(table):
            at = place[4 + n] - place[2]
            here_ref[jnp.where((at >= 0) & (at < lists), at, lists)] = n

    here = [here_ref[j] for j in range(lists)]
    total_rows = [ROWS * place[4 + table + n] for n in here]
    live = [n - place[3] for n in total_rows]

    @pl.when(core == place[1])
    def _():
        q_ref[...] = own_ref[...]

    @pl.when(core != place[1])
    def _():
        q_ref[...] = other_ref[...]

    queries = q_ref[:, :width]
    q_out[...] = queries.astype(jnp.float32).T.astype(jnp.bfloat16)
    info = q_ref[:, width:].astype(jnp.float32).T
    probes = info[0:PROBES, :]
    number = lax.broadcasted_iota(jnp.int32, (PROBES, tile), 0).astype(jnp.float32)
    target = jnp.sum(jnp.where(number == info[PROBES : PROBES + 1, :], probes, 0.0), axis=0, keepdims=True)
    raw_row = info[PROBES + 1 : PROBES + 2, :] * 64.0 + info[PROBES + 2 : PROBES + 3, :]
    code = jnp.full((1, tile), -1.0, jnp.float32)
    bias = []
    for j in range(lists):
        name = here[j].astype(jnp.float32)
        probed = jnp.max(jnp.where(probes == name, 1.0, 0.0), axis=0, keepdims=True)
        bias.append(jnp.where(probed > 0.0, 0.0, NEG_FILL))
        length = total_rows[j].astype(jnp.float32)
        row = raw_row - jnp.where(raw_row >= length, length, 0.0) - place[3].astype(jnp.float32)
        inside = (target == name) & (row >= 0.0) & (row < float(per))
        code = jnp.where(inside, row + float(j * per), code)
    code_ref[...] = code
    bias = columns_of(jnp.concatenate(bias, axis=0), tile)
    for j in range(lists):
        bias_ref[j] = lanes_of(bias[:, j : j + 1], tile)
    bias_ref[lists] = jnp.full((tile, LANES), NEG_FILL, jnp.float32)

    adapted = (
        queries.astype(jnp.float32) + jnp.dot(queries, w_ref[...], preferred_element_type=jnp.float32)
    ).astype(jnp.bfloat16)

    lane = lax.broadcasted_iota(jnp.int32, (tile, LANES), 1)
    blocks = per // LANES

    def matmul(j):
        raw = lax.dot_general(
            adapted, rows_ref[j], (((1,), (1,)), ((), ())), preferred_element_type=jnp.float32
        )
        top = None
        for b in range(blocks):
            which = jnp.where(live[j] > b * LANES, j, lists)
            piece = raw[:, b * LANES : (b + 1) * LANES] + bias_ref[which]
            s_ref[j % 2, :, b * LANES : (b + 1) * LANES] = piece
            top = piece if top is None else jnp.maximum(top, piece)
        return top

    def weigh(j, top):
        peak = lanes_of(jnp.max(top, axis=1, keepdims=True), tile) * factor
        total = None
        for b in range(blocks):
            weight = jnp.exp2(s_ref[j % 2, :, b * LANES : (b + 1) * LANES] * factor - peak)
            total = weight if total is None else total + weight
            at = j * per + b * LANES
            p_ref[:, at : at + LANES] = weight.astype(jnp.bfloat16)
        return peak, lanes_of(jnp.sum(total, axis=1, keepdims=True), tile)

    tops = jnp.full((tile, LANES), NEG_FILL, jnp.float32)
    sums = jnp.zeros((tile, LANES), jnp.float32)
    waiting = matmul(0)
    for j in range(lists):
        following = matmul(j + 1) if j + 1 < lists else None
        peak, total = weigh(j, waiting)
        tops = jnp.where(lane == j, peak, tops)
        sums = jnp.where(lane == j, total, sums)
        waiting = following
    tops = tops.T[0:lists, :]
    sums = sums.T[0:lists, :]
    tops_ref[...] = tops
    high = jnp.max(tops, axis=0, keepdims=True)
    stats_ref[0:1, :] = high
    stats_ref[1:2, :] = jnp.sum(sums * jnp.exp2(tops - high), axis=0, keepdims=True)


def back_kernel(stats_ref, code_ref, tops_ref, p_ref, rows_ref, *refs):
    out_ref, target_ref, g_ref, row_ref = refs[-4:]
    lists, per, width = rows_ref.shape
    tile = tops_ref.shape[1]
    share = columns_of(jnp.exp2(tops_ref[...] - stats_ref[0:1, :]), tile)
    acc = None
    for j in range(lists):
        part = lanes_of(share[:, j : j + 1], tile)
        for b in range(per // LANES):
            at = j * per + b * LANES
            g_ref[:, at : at + LANES] = (p_ref[:, at : at + LANES].astype(jnp.float32) * part).astype(jnp.bfloat16)
        out = jnp.dot(g_ref[:, j * per : (j + 1) * per], rows_ref[j], preferred_element_type=jnp.float32)
        acc = out if acc is None else acc + out
    out_ref[...] = acc

    row_ref[...] = jnp.zeros_like(row_ref)
    code = code_ref[...]
    index = lax.broadcasted_iota(jnp.int32, (1, tile), 1).astype(jnp.float32)
    sub = lax.broadcasted_iota(jnp.int32, (16, width), 0)
    keys = lists * per
    none = float(tile * keys)
    both = jnp.where(code >= 0.0, index * float(keys) + code, none)

    def first_after(last):
        return jnp.min(jnp.where(both > last, both, none))

    def step(found):
        at = found.astype(jnp.int32) // keys
        key = found.astype(jnp.int32) % keys
        group = rows_ref[key // per, pl.ds(pl.multiple_of((key % per) // 16 * 16, 16), 16), :]
        row = jnp.sum(jnp.where(sub == key % 16, group.astype(jnp.float32), 0.0), axis=0, keepdims=True)
        row_ref[pl.ds(at, 1), :] = row
        return first_after(found)

    lax.while_loop(lambda found: found < none, step, first_after(-1.0))
    target_ref[...] = row_ref[...].astype(jnp.bfloat16)


def scale_kernel(place, local_ref, whole_ref, out_ref, target_ref, scaled_ref):
    tile, width = out_ref.shape
    share = jnp.exp2(local_ref[0:1, :] - whole_ref[0:1, :]) / whole_ref[1:2, :]
    share = jnp.broadcast_to(share, (LANES, tile)).T
    for b in range(width // LANES):
        at = slice(b * LANES, (b + 1) * LANES)
        scaled_ref[:, at] = (
            (out_ref[:, at] * share - target_ref[:, at].astype(jnp.float32)) * (1.0 / math.sqrt(width))
        ).astype(jnp.bfloat16)


def adapter_kernel(other, place, q0, q1, q2, q3, b_ref, *refs):
    out_ref, q_ref = refs[-2:]
    half = b_ref.shape[0] // 4
    core = 1 - place[1] if other else place[1]
    for ahead, q in zip(ORDER, (q0, q1, q2, q3)):
        to = pl.multiple_of(lax.rem(place[0] + ahead, 4) * half, half)
        q_ref[:, pl.ds(to, half)] = q[:, pl.ds(pl.multiple_of(core * half, half), half)]
    total = jnp.dot(q_ref[...], b_ref[...], preferred_element_type=jnp.float32)
    if other:
        total = (total + refs[0][...]) * (1.0 / math.sqrt(8 * half))
    out_ref[...] = total


def merge_axis(stats, axis):
    chunk = stats.shape[1] // 4
    parts = [stats]
    for j in range(1, lax.axis_size(axis)):
        part = from_ahead(stats, axis, j)
        if axis == "z":
            at = [ORDER.index((ahead - j) % 4) for ahead in ORDER]
            part = jnp.concatenate([part[:, k * chunk : (k + 1) * chunk] for k in at], axis=1)
        parts.append(part)
    top = functools.reduce(jnp.maximum, [p[0] for p in parts])
    total = sum(p[1] * jnp.exp2(p[0] - top) for p in parts)
    return jnp.stack([top, total])


def all_steps(queries, adapter_w, index_rows, probes, list_slot, block_counts, target_raw):
    width = queries.shape[1]
    lists_here, rows_here = index_rows.shape[0], index_rows.shape[1]
    place_z, place_c = lax.axis_index("z"), lax.axis_index("core")
    place_y, place_x = lax.axis_index("y"), lax.axis_index("x")
    first_slot = (place_z * 2 + place_c) * lists_here
    first_row = (place_y * 4 + place_x) * rows_here
    list_length = rows_here * 16
    table = list_slot.shape[0]
    place = jnp.concatenate(
        [jnp.stack([place_z, place_c, first_slot, first_row]).astype(jnp.int32), list_slot, block_counts]
    )

    lane = jnp.arange(LANES, dtype=jnp.int32)[None, :]
    raw_row = lax.rem(target_raw, list_length)[:, None]
    info = jnp.pad(probes, ((0, 0), (0, LANES - PROBES)))
    info = jnp.where(lane == PROBES, lax.div(target_raw, list_length)[:, None], info)
    info = jnp.where(lane == PROBES + 1, lax.div(raw_row, 64), info)
    info = jnp.where(lane == PROBES + 2, lax.rem(raw_row, 64), info)
    packed = jnp.concatenate([queries, info.astype(jnp.bfloat16)], axis=1)
    packed, place = lax.optimization_barrier((packed, place))
    plane = spread_axes(packed, ("y", "x"))

    half = plane.shape[0]
    tile = 2 * half
    steps = 4
    count = steps * tile
    keys = lists_here * rows_here
    owns = [plane]
    for ahead in (1, 3):
        owns.append(from_ahead(plane, "z", ahead))
    weights, tops, stats, codes, gathered = [], [], [], [], []
    for i, ahead in enumerate(ORDER):
        if i == 1:
            held, codes[0] = lax.optimization_barrier((plane, codes[0]))
            owns.append(from_ahead(held, "z", 2))
        own = owns[i]
        other = from_ahead(own, "core", 1)
        call = pl.pallas_call(
            functools.partial(score_kernel, table),
            grid_spec=pltpu.PrefetchScalarGridSpec(
                num_scalar_prefetch=1,
                grid=(2,),
                in_specs=[
                    pl.BlockSpec((half, width + LANES), lambda i, *_: (0, 0)),
                    pl.BlockSpec((half, width + LANES), lambda i, *_: (0, 0)),
                    WHOLE,
                    WHOLE,
                ],
                out_specs=[
                    pl.BlockSpec((half, keys), lambda i, *_: (i, 0)),
                    pl.BlockSpec((lists_here, half), lambda i, *_: (0, i)),
                    pl.BlockSpec((2, half), lambda i, *_: (0, i)),
                    pl.BlockSpec((1, half), lambda i, *_: (0, i)),
                    pl.BlockSpec((width, half), lambda i, *_: (0, i)),
                ],
                scratch_shapes=[
                    pltpu.VMEM((half, width + LANES), jnp.bfloat16),
                    pltpu.VMEM((lists_here + 1, half, LANES), jnp.float32),
                    pltpu.VMEM((2, half, rows_here), jnp.float32),
                    pltpu.SMEM((lists_here + 1,), jnp.int32),
                ],
            ),
            out_shape=[
                jax.ShapeDtypeStruct((tile, keys), jnp.bfloat16),
                jax.ShapeDtypeStruct((lists_here, tile), jnp.float32),
                jax.ShapeDtypeStruct((2, tile), jnp.float32),
                jax.ShapeDtypeStruct((1, tile), jnp.float32),
                jax.ShapeDtypeStruct((width, tile), jnp.bfloat16),
            ],
            compiler_params=pltpu.CompilerParams(vmem_limit_bytes=12 << 20),
            cost_estimate=pl.CostEstimate(
                flops=2 * tile * width * (keys + width), bytes_accessed=tile * keys * 2, transcendentals=tile * keys
            ),
            name="scores",
        )
        outs = call(place, own, other, adapter_w, index_rows)
        for kept, value in zip((weights, tops, stats, codes, gathered), outs):
            kept.append(value)

    out_all = target_all = None
    for i in range(steps):
        rest = [] if i == 0 else [out_all, target_all]
        call = pl.pallas_call(
            back_kernel,
            grid=(2,),
            in_specs=[
                pl.BlockSpec((2, half), lambda k: (0, k)),
                pl.BlockSpec((1, half), lambda k: (0, k)),
                pl.BlockSpec((lists_here, half), lambda k: (0, k)),
                pl.BlockSpec((half, keys), lambda k: (k, 0)),
                WHOLE,
            ]
            + [pl.BlockSpec(memory_space=pl.ANY)] * len(rest),
            out_specs=[pl.BlockSpec((half, width), lambda k, i=i: (2 * i + k, 0))] * 2,
            out_shape=[
                jax.ShapeDtypeStruct((count, width), jnp.float32),
                jax.ShapeDtypeStruct((count, width), jnp.bfloat16),
            ],
            scratch_shapes=[
                pltpu.VMEM((half, keys), jnp.bfloat16),
                pltpu.VMEM((half, width), jnp.float32),
            ],
            input_output_aliases={5: 0, 6: 1} if rest else {},
            compiler_params=pltpu.CompilerParams(vmem_limit_bytes=24 << 20),
            cost_estimate=pl.CostEstimate(
                flops=2 * tile * width * keys, bytes_accessed=tile * keys * 2, transcendentals=0
            ),
            name="backs",
        )
        out_all, target_all = call(stats[i], codes[i], tops[i], weights[i], index_rows, *rest)

    local_stats = jnp.concatenate(stats, axis=1)
    whole_stats = local_stats
    for axis in ("core", "x", "y", "z"):
        whole_stats = merge_axis(whole_stats, axis)

    def scaled(other):
        def part(i, place):
            return 2 * i + (1 - place[1] if other else place[1])

        return pl.pallas_call(
            scale_kernel,
            grid_spec=pltpu.PrefetchScalarGridSpec(
                num_scalar_prefetch=1,
                grid=(steps,),
                in_specs=[
                    pl.BlockSpec((2, half), lambda i, place: (0, part(i, place))),
                    pl.BlockSpec((2, half), lambda i, place: (0, part(i, place))),
                    pl.BlockSpec((half, width), lambda i, place: (part(i, place), 0)),
                    pl.BlockSpec((half, width), lambda i, place: (part(i, place), 0)),
                ],
                out_specs=pl.BlockSpec(
                    (half, width), lambda i, place: (lax.rem(place[0] + chunk_of(i), 4), 0)
                ),
            ),
            out_shape=jax.ShapeDtypeStruct((count // 2, width), jnp.bfloat16),
            compiler_params=pltpu.CompilerParams(vmem_limit_bytes=12 << 20),
            cost_estimate=pl.CostEstimate(
                flops=2 * count * width, bytes_accessed=count * width * 4, transcendentals=0
            ),
            name="scaled",
        )(place, local_stats, whole_stats, out_all, target_all)

    theirs = scaled(True)
    received = from_ahead(theirs, "core", 1)
    mine = scaled(False)
    merged = (mine.astype(jnp.float32) + received.astype(jnp.float32)).astype(jnp.bfloat16)
    pieces = lax.all_to_all(merged, CHIPS, split_axis=0, concat_axis=0, tiled=True)
    back = jnp.sum(pieces.reshape(-1, queries.shape[0], width).astype(jnp.float32), axis=0)
    back_low = back.astype(jnp.bfloat16)
    query_grad = (
        back
        + lax.dot_general(back_low, adapter_w, (((1,), (1,)), ((), ())), preferred_element_type=jnp.float32)
    ).astype(jnp.bfloat16)
    b_own = spread_axes(back_low, CHIPS)
    b_other = from_ahead(b_own, "core", 1)
    third = width // 3
    column = pl.BlockSpec((third, tile), lambda i, place: (i, 0))
    block = pl.BlockSpec((third, width), lambda i, place: (i, 0))

    def product(other, *rest):
        return pl.pallas_call(
            functools.partial(adapter_kernel, other),
            grid_spec=pltpu.PrefetchScalarGridSpec(
                num_scalar_prefetch=1,
                grid=(3,),
                in_specs=[column, column, column, column, WHOLE] + [block] * (len(rest) - 1),
                out_specs=block,
                scratch_shapes=[pltpu.VMEM((third, count // 2), jnp.bfloat16)],
            ),
            out_shape=jax.ShapeDtypeStruct((width, width), jnp.float32),
            compiler_params=pltpu.CompilerParams(vmem_limit_bytes=16 << 20),
            cost_estimate=pl.CostEstimate(
                flops=count * width * width, bytes_accessed=count * width * 2, transcendentals=0
            ),
            name="adapter",
        )(place, *gathered, *rest)

    partial = product(False, b_own)
    adapter_grad = product(True, b_other, partial)
    return (query_grad, adapter_grad)


def solution(mesh):
    split = Mesh(mesh.devices.reshape(SIZES), AXES)
    placed = (
        P(AXES, None),
        P(),
        P(("z", "core"), ("y", "x"), None),
        P(AXES, None),
        P(),
        P(),
        P(AXES),
    )
    return jax.shard_map(
        all_steps,
        mesh=split,
        in_specs=placed,
        out_specs=(P(AXES, None), P()),
        check_vma=False,
    )
```

```python
import functools
import math

import jax
import jax.numpy as jnp
from jax import lax
from jax.experimental import pallas as pl
from jax.experimental.pallas import tpu as pltpu
from jax.sharding import Mesh
from jax.sharding import PartitionSpec as P

ROWS = 128
NEG_FILL = -1e30
LANES = 128
PROBES = 16
SIZES = (4, 2, 4, 4)
AXES = ("z", "core", "y", "x")
CHIPS = ("z", "y", "x")
ORDER = (0, 1, 3, 2)
COVER = 5000000000
LOG2E = 1.4426950408889634
WHOLE = pl.BlockSpec(memory_space=pltpu.VMEM)


def from_ahead(value, axis, step):
    size = lax.axis_size(axis)
    return lax.ppermute(value, axis, [((i + step) % size, i) for i in range(size)])


def chunk_of(i):
    return jnp.where(i < 2, i, 5 - i)


def spread_axes(value, axes):
    size = lax.axis_size(axes)
    spread = jnp.broadcast_to(value[None], (size,) + value.shape).reshape((-1,) + value.shape[1:])
    return lax.all_to_all(spread, axes, split_axis=0, concat_axis=0, tiled=True)


def lanes_of(column, tile):
    return jnp.broadcast_to(column, (tile, LANES))


def columns_of(rows, tile):
    return jnp.concatenate([rows, jnp.zeros((LANES - rows.shape[0], tile), jnp.float32)], axis=0).T


def score_kernel(
    table, place, own_ref, other_ref, w_ref, rows_ref, _,
    p_ref, tops_ref, stats_ref, code_ref, q_out, q_ref, bias_ref, s_ref, here_ref,
):
    width = w_ref.shape[0]
    tile = own_ref.shape[0]
    lists, per = rows_ref.shape[0], rows_ref.shape[1]
    factor = LOG2E / math.sqrt(width)
    core = pl.program_id(0)

    @pl.when(core == 0)
    def _():
        for n in range(table):
            at = place[4 + n] - place[2]
            here_ref[jnp.where((at >= 0) & (at < lists), at, lists)] = n

    here = [here_ref[j] for j in range(lists)]
    total_rows = [ROWS * place[4 + table + n] for n in here]
    live = [n - place[3] for n in total_rows]

    @pl.when(core == place[1])
    def _():
        q_ref[...] = own_ref[...]

    @pl.when(core != place[1])
    def _():
        q_ref[...] = other_ref[...]

    queries = q_ref[:, :width]
    q_out[...] = queries.astype(jnp.float32).T.astype(jnp.bfloat16)
    info = q_ref[:, width:].astype(jnp.float32).T
    probes = info[0:PROBES, :]
    number = lax.broadcasted_iota(jnp.int32, (PROBES, tile), 0).astype(jnp.float32)
    target = jnp.sum(jnp.where(number == info[PROBES : PROBES + 1, :], probes, 0.0), axis=0, keepdims=True)
    raw_row = info[PROBES + 1 : PROBES + 2, :] * 64.0 + info[PROBES + 2 : PROBES + 3, :]
    code = jnp.full((1, tile), -1.0, jnp.float32)
    bias = []
    for j in range(lists):
        name = here[j].astype(jnp.float32)
        probed = jnp.max(jnp.where(probes == name, 1.0, 0.0), axis=0, keepdims=True)
        bias.append(jnp.where(probed > 0.0, 0.0, NEG_FILL))
        length = total_rows[j].astype(jnp.float32)
        row = raw_row - jnp.where(raw_row >= length, length, 0.0) - place[3].astype(jnp.float32)
        inside = (target == name) & (row >= 0.0) & (row < float(per))
        code = jnp.where(inside, row + float(j * per), code)
    code_ref[...] = code
    bias = columns_of(jnp.concatenate(bias, axis=0), tile)
    for j in range(lists):
        bias_ref[j] = lanes_of(bias[:, j : j + 1], tile)
    bias_ref[lists] = jnp.full((tile, LANES), NEG_FILL, jnp.float32)

    adapted = (
        queries.astype(jnp.float32) + jnp.dot(queries, w_ref[...], preferred_element_type=jnp.float32)
    ).astype(jnp.bfloat16)

    lane = lax.broadcasted_iota(jnp.int32, (tile, LANES), 1)
    blocks = per // LANES

    def matmul(j):
        raw = lax.dot_general(
            adapted, rows_ref[j], (((1,), (1,)), ((), ())), preferred_element_type=jnp.float32
        )
        top = None
        for b in range(blocks):
            which = jnp.where(live[j] > b * LANES, j, lists)
            piece = raw[:, b * LANES : (b + 1) * LANES] + bias_ref[which]
            s_ref[j % 2, :, b * LANES : (b + 1) * LANES] = piece
            top = piece if top is None else jnp.maximum(top, piece)
        return top

    def weigh(j, top):
        peak = lanes_of(jnp.max(top, axis=1, keepdims=True), tile) * factor
        total = None
        for b in range(blocks):
            weight = jnp.exp2(s_ref[j % 2, :, b * LANES : (b + 1) * LANES] * factor - peak)
            total = weight if total is None else total + weight
            at = j * per + b * LANES
            p_ref[:, at : at + LANES] = weight.astype(jnp.bfloat16)
        return peak, lanes_of(jnp.sum(total, axis=1, keepdims=True), tile)

    tops = jnp.full((tile, LANES), NEG_FILL, jnp.float32)
    sums = jnp.zeros((tile, LANES), jnp.float32)
    waiting = matmul(0)
    for j in range(lists):
        following = matmul(j + 1) if j + 1 < lists else None
        peak, total = weigh(j, waiting)
        tops = jnp.where(lane == j, peak, tops)
        sums = jnp.where(lane == j, total, sums)
        waiting = following
    tops = tops.T[0:lists, :]
    sums = sums.T[0:lists, :]
    tops_ref[...] = tops
    high = jnp.max(tops, axis=0, keepdims=True)
    stats_ref[0:1, :] = high
    stats_ref[1:2, :] = jnp.sum(sums * jnp.exp2(tops - high), axis=0, keepdims=True)


def turn_kernel(plane_ref, out_ref):
    out_ref[...] = plane_ref[...].astype(jnp.float32).T.astype(jnp.bfloat16)


def back_kernel(stats_ref, code_ref, tops_ref, p_ref, rows_ref, *refs):
    out_ref, target_ref, g_ref, row_ref = refs[-4:]
    lists, per, width = rows_ref.shape
    tile = tops_ref.shape[1]
    share = columns_of(jnp.exp2(tops_ref[...] - stats_ref[0:1, :]), tile)
    acc = None
    for j in range(lists):
        part = lanes_of(share[:, j : j + 1], tile)
        for b in range(per // LANES):
            at = j * per + b * LANES
            g_ref[:, at : at + LANES] = (p_ref[:, at : at + LANES].astype(jnp.float32) * part).astype(jnp.bfloat16)
        out = jnp.dot(g_ref[:, j * per : (j + 1) * per], rows_ref[j], preferred_element_type=jnp.float32)
        acc = out if acc is None else acc + out
    out_ref[...] = acc

    row_ref[...] = jnp.zeros_like(row_ref)
    code = code_ref[...]
    index = lax.broadcasted_iota(jnp.int32, (1, tile), 1).astype(jnp.float32)
    sub = lax.broadcasted_iota(jnp.int32, (16, width), 0)
    keys = lists * per
    none = float(tile * keys)
    both = jnp.where(code >= 0.0, index * float(keys) + code, none)

    def first_after(last):
        return jnp.min(jnp.where(both > last, both, none))

    def step(found):
        at = found.astype(jnp.int32) // keys
        key = found.astype(jnp.int32) % keys
        group = rows_ref[key // per, pl.ds(pl.multiple_of((key % per) // 16 * 16, 16), 16), :]
        row = jnp.sum(jnp.where(sub == key % 16, group.astype(jnp.float32), 0.0), axis=0, keepdims=True)
        row_ref[pl.ds(at, 1), :] = row
        return first_after(found)

    lax.while_loop(lambda found: found < none, step, first_after(-1.0))
    target_ref[...] = row_ref[...].astype(jnp.bfloat16)


def scale_kernel(place, local_ref, whole_ref, out_ref, target_ref, scaled_ref):
    tile, width = out_ref.shape
    share = jnp.exp2(local_ref[0:1, :] - whole_ref[0:1, :]) / whole_ref[1:2, :]
    share = jnp.broadcast_to(share, (LANES, tile)).T
    for b in range(width // LANES):
        at = slice(b * LANES, (b + 1) * LANES)
        scaled_ref[:, at] = (
            (out_ref[:, at] * share - target_ref[:, at].astype(jnp.float32)) * (1.0 / math.sqrt(width))
        ).astype(jnp.bfloat16)


def adapter_kernel(other, place, q0, q1, q2, q3, b_ref, *refs):
    out_ref, q_ref = refs[-2:]
    half = b_ref.shape[0] // 4
    core = 1 - place[1] if other else place[1]
    for ahead, q in zip(ORDER, (q0, q1, q2, q3)):
        to = pl.multiple_of(lax.rem(place[0] + ahead, 4) * half, half)
        q_ref[:, pl.ds(to, half)] = q[:, pl.ds(pl.multiple_of(core * half, half), half)]
    total = jnp.dot(q_ref[...], b_ref[...], preferred_element_type=jnp.float32)
    if other:
        total = (total + refs[0][...]) * (1.0 / math.sqrt(8 * half))
    out_ref[...] = total


def merge_axis(stats, axis):
    chunk = stats.shape[1] // 4
    parts = [stats]
    for j in range(1, lax.axis_size(axis)):
        part = from_ahead(stats, axis, j)
        if axis == "z":
            at = [ORDER.index((ahead - j) % 4) for ahead in ORDER]
            part = jnp.concatenate([part[:, k * chunk : (k + 1) * chunk] for k in at], axis=1)
        parts.append(part)
    top = functools.reduce(jnp.maximum, [p[0] for p in parts])
    total = sum(p[1] * jnp.exp2(p[0] - top) for p in parts)
    return jnp.stack([top, total])


def all_steps(queries, adapter_w, index_rows, probes, list_slot, block_counts, target_raw):
    width = queries.shape[1]
    lists_here, rows_here = index_rows.shape[0], index_rows.shape[1]
    place_z, place_c = lax.axis_index("z"), lax.axis_index("core")
    place_y, place_x = lax.axis_index("y"), lax.axis_index("x")
    first_slot = (place_z * 2 + place_c) * lists_here
    first_row = (place_y * 4 + place_x) * rows_here
    list_length = rows_here * 16
    table = list_slot.shape[0]
    place = jnp.concatenate(
        [jnp.stack([place_z, place_c, first_slot, first_row]).astype(jnp.int32), list_slot, block_counts]
    )

    lane = jnp.arange(LANES, dtype=jnp.int32)[None, :]
    raw_row = lax.rem(target_raw, list_length)[:, None]
    info = jnp.pad(probes, ((0, 0), (0, LANES - PROBES)))
    info = jnp.where(lane == PROBES, lax.div(target_raw, list_length)[:, None], info)
    info = jnp.where(lane == PROBES + 1, lax.div(raw_row, 64), info)
    info = jnp.where(lane == PROBES + 2, lax.rem(raw_row, 64), info)
    packed = jnp.concatenate([queries, info.astype(jnp.bfloat16)], axis=1)
    packed, place = lax.optimization_barrier((packed, place))
    plane = spread_axes(packed, ("y", "x"))

    half = plane.shape[0]
    tile = 2 * half
    steps = 4
    count = steps * tile
    keys = lists_here * rows_here
    turned = pl.pallas_call(
        turn_kernel,
        grid=(1,),
        in_specs=[pl.BlockSpec((half, LANES), lambda k: (0, width // LANES))],
        out_specs=pl.BlockSpec((LANES, half), lambda k: (0, 0)),
        out_shape=jax.ShapeDtypeStruct((LANES, half), jnp.bfloat16),
        compiler_params=pltpu.CompilerParams(vmem_limit_bytes=4 << 20),
        cost_estimate=pl.CostEstimate(flops=COVER, bytes_accessed=half * LANES * 4, transcendentals=0),
        name="turn",
    )(plane)
    owns = [plane]
    for ahead in (1, 3):
        owns.append(from_ahead(plane, "z", ahead))
    weights, tops, stats, codes, gathered = [], [], [], [], []
    for i, ahead in enumerate(ORDER):
        if i == 1:
            held, codes[0], owns[1] = lax.optimization_barrier((plane, codes[0], owns[1]))
            owns.append(from_ahead(held, "z", 2))
        own = owns[i]
        other = from_ahead(own, "core", 1)
        call = pl.pallas_call(
            functools.partial(score_kernel, table),
            grid_spec=pltpu.PrefetchScalarGridSpec(
                num_scalar_prefetch=1,
                grid=(2,),
                in_specs=[
                    pl.BlockSpec((half, width + LANES), lambda i, *_: (0, 0)),
                    pl.BlockSpec((half, width + LANES), lambda i, *_: (0, 0)),
                    WHOLE,
                    WHOLE,
                    pl.BlockSpec(memory_space=pl.ANY),
                ],
                out_specs=[
                    pl.BlockSpec((half, keys), lambda i, *_: (i, 0)),
                    pl.BlockSpec((lists_here, half), lambda i, *_: (0, i)),
                    pl.BlockSpec((2, half), lambda i, *_: (0, i)),
                    pl.BlockSpec((1, half), lambda i, *_: (0, i)),
                    pl.BlockSpec((width, half), lambda i, *_: (0, i)),
                ],
                scratch_shapes=[
                    pltpu.VMEM((half, width + LANES), jnp.bfloat16),
                    pltpu.VMEM((lists_here + 1, half, LANES), jnp.float32),
                    pltpu.VMEM((2, half, rows_here), jnp.float32),
                    pltpu.SMEM((lists_here + 1,), jnp.int32),
                ],
            ),
            out_shape=[
                jax.ShapeDtypeStruct((tile, keys), jnp.bfloat16),
                jax.ShapeDtypeStruct((lists_here, tile), jnp.float32),
                jax.ShapeDtypeStruct((2, tile), jnp.float32),
                jax.ShapeDtypeStruct((1, tile), jnp.float32),
                jax.ShapeDtypeStruct((width, tile), jnp.bfloat16),
            ],
            compiler_params=pltpu.CompilerParams(vmem_limit_bytes=12 << 20),
            cost_estimate=pl.CostEstimate(
                flops=2 * tile * width * (keys + width), bytes_accessed=tile * keys * 2, transcendentals=tile * keys
            ),
            name="scores",
        )
        outs = call(place, own, other, adapter_w, index_rows, turned)
        for kept, value in zip((weights, tops, stats, codes, gathered), outs):
            kept.append(value)

    out_all = target_all = None
    for i in range(steps):
        rest = [] if i == 0 else [out_all, target_all]
        call = pl.pallas_call(
            back_kernel,
            grid=(2,),
            in_specs=[
                pl.BlockSpec((2, half), lambda k: (0, k)),
                pl.BlockSpec((1, half), lambda k: (0, k)),
                pl.BlockSpec((lists_here, half), lambda k: (0, k)),
                pl.BlockSpec((half, keys), lambda k: (k, 0)),
                WHOLE,
            ]
            + [pl.BlockSpec(memory_space=pl.ANY)] * len(rest),
            out_specs=[pl.BlockSpec((half, width), lambda k, i=i: (2 * i + k, 0))] * 2,
            out_shape=[
                jax.ShapeDtypeStruct((count, width), jnp.float32),
                jax.ShapeDtypeStruct((count, width), jnp.bfloat16),
            ],
            scratch_shapes=[
                pltpu.VMEM((half, keys), jnp.bfloat16),
                pltpu.VMEM((half, width), jnp.float32),
            ],
            input_output_aliases={5: 0, 6: 1} if rest else {},
            compiler_params=pltpu.CompilerParams(vmem_limit_bytes=24 << 20),
            cost_estimate=pl.CostEstimate(
                flops=2 * tile * width * keys, bytes_accessed=tile * keys * 2, transcendentals=0
            ),
            name="backs",
        )
        out_all, target_all = call(stats[i], codes[i], tops[i], weights[i], index_rows, *rest)

    local_stats = jnp.concatenate(stats, axis=1)
    whole_stats = local_stats
    for axis in ("core", "x", "y", "z"):
        whole_stats = merge_axis(whole_stats, axis)

    def scaled(other):
        def part(i, place):
            return 2 * i + (1 - place[1] if other else place[1])

        return pl.pallas_call(
            scale_kernel,
            grid_spec=pltpu.PrefetchScalarGridSpec(
                num_scalar_prefetch=1,
                grid=(steps,),
                in_specs=[
                    pl.BlockSpec((2, half), lambda i, place: (0, part(i, place))),
                    pl.BlockSpec((2, half), lambda i, place: (0, part(i, place))),
                    pl.BlockSpec((half, width), lambda i, place: (part(i, place), 0)),
                    pl.BlockSpec((half, width), lambda i, place: (part(i, place), 0)),
                ],
                out_specs=pl.BlockSpec(
                    (half, width), lambda i, place: (lax.rem(place[0] + chunk_of(i), 4), 0)
                ),
            ),
            out_shape=jax.ShapeDtypeStruct((count // 2, width), jnp.bfloat16),
            compiler_params=pltpu.CompilerParams(vmem_limit_bytes=12 << 20),
            cost_estimate=pl.CostEstimate(
                flops=2 * count * width, bytes_accessed=count * width * 4, transcendentals=0
            ),
            name="scaled",
        )(place, local_stats, whole_stats, out_all, target_all)

    theirs = scaled(True)
    received = from_ahead(theirs, "core", 1)
    mine = scaled(False)
    merged = (mine.astype(jnp.float32) + received.astype(jnp.float32)).astype(jnp.bfloat16)
    pieces = lax.all_to_all(merged, CHIPS, split_axis=0, concat_axis=0, tiled=True)
    back = jnp.sum(pieces.reshape(-1, queries.shape[0], width).astype(jnp.float32), axis=0)
    back_low = back.astype(jnp.bfloat16)
    query_grad = (
        back
        + lax.dot_general(back_low, adapter_w, (((1,), (1,)), ((), ())), preferred_element_type=jnp.float32)
    ).astype(jnp.bfloat16)
    b_own = spread_axes(back_low, CHIPS)
    b_other = from_ahead(b_own, "core", 1)
    third = width // 3
    column = pl.BlockSpec((third, tile), lambda i, place: (i, 0))
    block = pl.BlockSpec((third, width), lambda i, place: (i, 0))

    def product(other, *rest):
        return pl.pallas_call(
            functools.partial(adapter_kernel, other),
            grid_spec=pltpu.PrefetchScalarGridSpec(
                num_scalar_prefetch=1,
                grid=(3,),
                in_specs=[column, column, column, column, WHOLE] + [block] * (len(rest) - 1),
                out_specs=block,
                scratch_shapes=[pltpu.VMEM((third, count // 2), jnp.bfloat16)],
            ),
            out_shape=jax.ShapeDtypeStruct((width, width), jnp.float32),
            compiler_params=pltpu.CompilerParams(vmem_limit_bytes=16 << 20),
            cost_estimate=pl.CostEstimate(
                flops=count * width * width, bytes_accessed=count * width * 2, transcendentals=0
            ),
            name="adapter",
        )(place, *gathered, *rest)

    partial = product(False, b_own)
    adapter_grad = product(True, b_other, partial)
    return (query_grad, adapter_grad)


def solution(mesh):
    split = Mesh(mesh.devices.reshape(SIZES), AXES)
    placed = (
        P(AXES, None),
        P(),
        P(("z", "core"), ("y", "x"), None),
        P(AXES, None),
        P(),
        P(),
        P(AXES),
    )
    return jax.shard_map(
        all_steps,
        mesh=split,
        in_specs=placed,
        out_specs=(P(AXES, None), P()),
        check_vma=False,
    )
```
